256 devices in a mesh: replica: 64 (over z, x, core), tensor: 4 (over y).
Axes of the slice: x: 4, y: 4, z: 8, core: 2. Of those that a mesh axis runs over, the one named last changes fastest.
Arguments:
- hidden_input: bfloat16 [4096, 3584], P('replica', 'tensor'), may hold values from -6 to 6
- queries: bfloat16 [4096, 2048], P('replica', 'tensor'), may hold values from -8 to 8
- prompt_cache: bfloat16 [256, 2, 2048, 1024], P('replica', None, None, 'tensor'), may hold values from -8 to 8
- suffix_cache: bfloat16 [4096, 2, 64, 1024], P('replica', None, None, 'tensor'), may hold values from -6 to 6
- owner_replica: int32 [4096, 1], P('replica'), may hold values from 0 to 63; in each aligned block of 64 rows (0 to 63, 64 to 127, ...) at most 2 rows name the same one
- group_slot: int32 [4096], P('replica'), may hold values from 0 to 3
- prompt_length: int32 [256], P('replica'), may hold values from 256 to 2048
- suffix_length: int32 [4096], P('replica'), may hold values from 1 to 64
- output_weight: bfloat16 [2048, 3584], P('tensor'), may hold values from -0.1875 to 0.1875
- post_gain: float32 [3584], P('tensor'), may hold values from 0.1 to 1.9
Outputs:
- hidden_output: bfloat16 [4096, 3584], P('replica', 'tensor')
The draws below stay inside these ranges and needn't reach their ends.
Inputs may be any that keep to these rules, and one draw needn't show every extreme that they name: `owner_replica`: among the 64 requests of one replica, no owner replica is named more than 2 times.
All inputs are finite; a program needn't handle non-finite values.
Results may differ from the reference program's by a relative error of at most 0.0048.
Values may be sent and summed in bfloat16 or wider, within the bound.
A program may use at most 128 MiB of HBM per device.

```python
import math
import jax
import jax.numpy as jnp
import numpy as np
from jax import lax

D = 3584
HD = 256
QH = 8
KVH = 4
P_SIZE = 2048
S = 64
REQ_DEV = 64
G_DEV = 4
CAP = 2
REQUESTS = 4096
GROUPS = 256
N_REPLICA = 64


def shared_direction(key):
    signs = jax.random.bernoulli(jax.random.fold_in(key, 7), 0.5, (KVH, HD))
    return jnp.where(signs, jnp.float32(1.0), jnp.float32(-1.0))


def background_draw(key, shape):
    return jnp.clip(jax.random.normal(key, shape, jnp.float32), -6.0, 6.0)


def draw_queries(key, part):
    direction = shared_direction(key)
    background = background_draw(jax.random.fold_in(key, 11), (REQUESTS, QH, HD))
    chosen = jax.random.randint(jax.random.fold_in(key, 13), (REQUESTS, 1, 1), 0, 4) == 0
    strength = jax.random.uniform(jax.random.fold_in(key, 17), (REQUESTS, QH, 1), jnp.float32, 8.0, 10.0) / HD ** 0.25
    head_index = jnp.arange(QH) // (QH // KVH)
    head_direction = direction[head_index]
    aligned = strength * head_direction[None, :, :]
    result = jnp.where(chosen, aligned, background)
    return result.reshape(REQUESTS, QH * HD).astype(jnp.bfloat16)


def draw_prompt_cache(key, part):
    direction = shared_direction(key)
    background = background_draw(jax.random.fold_in(key, 19), (GROUPS, 2, P_SIZE, KVH, HD))
    special_spots = jax.random.randint(jax.random.fold_in(key, 23), (GROUPS, 3), 0, max(P_SIZE // 8, 1))
    positions = jnp.arange(P_SIZE)
    special = jnp.any(positions[None, None, :] == special_spots[:, :, None], axis=1)
    strength = jax.random.uniform(jax.random.fold_in(key, 29), (GROUPS, P_SIZE, KVH, 1), jnp.float32, 8.0, 14.0) / HD ** 0.25
    aligned = strength * direction[None, None, :, :]
    key_part = jnp.where(special[:, :, None, None], aligned, background[:, 0])
    value_part = background[:, 1]
    result = jnp.stack([key_part, value_part], axis=1)
    return result.reshape(GROUPS, 2, P_SIZE, KVH * HD).astype(jnp.bfloat16)


def plant(values, rng, low, high):
    place = [jax.random.randint(jax.random.fold_in(rng, axis), (), 0, length) for axis, length in enumerate(values.shape)]
    longest = values.shape.index(max(values.shape))
    beside = place[:longest] + [(place[longest] + 1) % values.shape[longest]] + place[longest + 1:]
    return values.at[tuple(place)].set(low).at[tuple(beside)].set(high)


def strengthened(entries, own_key, source, target, blocks, factor):
    def block_of(position):
        return (jnp.arange(entries.shape[position]) // (entries.shape[position] // blocks)).reshape((-1,) + (1,) * (entries.ndim - 1 - position))

    one_side = jax.random.permutation(own_key, blocks)[block_of(target)]
    second = (block_of(target) + blocks // 2) % blocks
    return jnp.where((block_of(source) == one_side) | (block_of(source) == second), factor * entries, entries)


def level_of(stream_key, extent, pieces, low, largest):
    level, own = 1.0, jax.random.fold_in(stream_key, 6)
    for position, blocks in pieces:
        draws = jnp.exp(jax.random.uniform(jax.random.fold_in(own, position), (blocks,), jnp.float32, low / len(pieces), largest / len(pieces)))
        level = level * jnp.repeat(draws, extent[position] // blocks).reshape([-1 if axis == position else 1 for axis in range(len(extent))])
    return level


def shared_out(own_key, own, number, rows, number_of, top, reach, slope):
    ranking = jax.random.permutation(own_key, number_of)
    heavy_load, ordinary = portions_of(number_of, rows * top, reach, slope, True), portions_of(number_of, rows * top, reach, slope, False)
    places = jnp.arange(number_of)

    def named(tallies, rotation):
        used = int((tallies > 0).sum())
        fixed = max(1, used // 4)
        passed = fixed + (places - fixed + rotation * (used - fixed)) % max(1, number_of - fixed)
        return jnp.zeros((number_of,), jnp.int32).at[ranking[jnp.where(places < fixed, places, passed)]].set(jnp.asarray(tallies, jnp.int32))

    tallies = jnp.where(number % 4 == 0, named(heavy_load, number // 4), named(ordinary, number - number // 4 - 1))
    mixed = jax.random.permutation(jax.random.fold_in(own, 3), number_of)
    giver, taker = mixed[0:number_of // 2 * 2:2], mixed[1:number_of // 2 * 2:2]
    slack = jnp.minimum(tallies[giver] - 1, reach - tallies[taker]) // 2
    slack = jnp.where((giver == ranking[0]) | (taker == ranking[0]) | (tallies[taker] == 0), 0, jnp.maximum(slack, 0))
    passed = jax.random.randint(jax.random.fold_in(own, 4), (number_of // 2,), 0, 1 << 20) % (slack + 1)
    tallies = tallies.at[giver].add(-passed).at[taker].add(passed)
    items = jnp.searchsorted(jnp.cumsum(tallies), jnp.arange(rows * top), side="right").astype(jnp.int32)
    table = items.reshape(top, rows).T
    table = table[jax.random.permutation(jax.random.fold_in(own, 1), rows)]
    rotation = jax.random.randint(jax.random.fold_in(own, 2), (rows, 1), 0, top)
    return jnp.take_along_axis(table, (jnp.arange(top)[None, :] + rotation) % top, axis=1)


def portions_of(count, total, limit, skew, full):
    portions = [(1 << 20) // math.isqrt(rank ** skew) + 1 for rank in range(1, count + 1)]
    largest = limit if full else min(limit, max(-(-total // count), total * portions[0] // sum(portions)))
    least = 1 if total - largest >= count - 1 else 0
    holding, rest = [largest] + [least] * (count - 1), total - largest - least * (count - 1)
    while rest > 0:
        movable = [i for i in range(1, count) if holding[i] < largest] or [i for i in range(1, count) if holding[i] < limit]
        whole, remaining = sum([portions[i] for i in movable]), rest
        for i in movable:
            addition = min(limit - holding[i], max(1, remaining * portions[i] // whole), rest)
            holding[i] = holding[i] + addition
            rest = rest - addition
    return np.array(holding)


def scatter_about(rng, extent, deviation, limit, split=(), held_as=jnp.bfloat16):
    level = level_of(rng, extent, split, -0.22, 0.18) if split else 1.0
    entries = jax.random.normal(rng, extent, jnp.float32) * deviation * level
    return jnp.minimum(jnp.maximum(entries, -limit), limit).astype(held_as)


def gaussian_with(own_key, shape, spread, reach, pieces, heavy, kind=jnp.bfloat16):
    entries = spread * jax.random.normal(own_key, shape, jnp.float32)
    if pieces:
        entries = entries * level_of(own_key, shape, pieces, -0.22, 0.18)
    return jnp.clip(strengthened(entries, jax.random.fold_in(own_key, 3), *heavy), -reach, reach).astype(kind)


def setup_inputs(seed: int = 0) -> dict:
    keys = jax.random.split(jax.random.key(seed), 11)
    hidden_input = scatter_about(keys[0], (REQUESTS, D), 1.0, 6.0, ((0, 64), (1, 4)))
    queries = draw_queries(jax.random.fold_in(keys[10], 71), 0)
    prompt_cache = draw_prompt_cache(jax.random.fold_in(keys[10], 71), 0)
    suffix_cache = scatter_about(keys[3], (REQUESTS, 2, S, KVH * HD), 1.0, 6.0, ((0, 64), (3, 4)))
    owner_replica_keys = jax.random.split(jax.random.fold_in(keys[4], 1), REQUESTS // REQ_DEV)
    owner_replica_turns = jax.random.permutation(jax.random.fold_in(keys[4], 3), REQUESTS // REQ_DEV)
    owner_replica = jax.vmap(lambda own, number: shared_out(jax.random.fold_in(keys[4], 2), own, number, REQ_DEV, N_REPLICA, 1, CAP, 2))(owner_replica_keys, owner_replica_turns).reshape((REQUESTS, 1))
    group_slot = plant(jax.random.randint(keys[5], (REQUESTS,), 0, G_DEV), jax.random.fold_in(keys[5], 1), 0, G_DEV - 1).astype(jnp.int32)
    prompt_length = plant(jax.random.randint(keys[6], (GROUPS,), P_SIZE // 8, P_SIZE + 1), jax.random.fold_in(keys[6], 1), P_SIZE // 8, P_SIZE).astype(jnp.int32)
    suffix_length = plant(jax.random.randint(keys[7], (REQUESTS,), 1, S + 1), jax.random.fold_in(keys[7], 1), 1, S).astype(jnp.int32)
    output_weight = gaussian_with(keys[8], (QH * HD, D), (QH * HD) ** -0.5, 0.1875, ((0, 4),), (0, 1, 4, 2.0))
    post_gain = jnp.clip(1.0 + 0.18 * jax.random.normal(keys[9], (D,), jnp.float32), 0.1, 1.9)
    return {"hidden_input": hidden_input, "queries": queries, "prompt_cache": prompt_cache, "suffix_cache": suffix_cache, "owner_replica": owner_replica, "group_slot": group_slot, "prompt_length": prompt_length, "suffix_length": suffix_length, "output_weight": output_weight, "post_gain": post_gain}


softcap = 50.0
epsilon = 1e-06

def partial_attend(heads, cache_rows, live_length, head_map):
    window = cache_rows.shape[1]
    key_rows = cache_rows[0].astype(jnp.float32).reshape(window, KVH, HD)[:, head_map]
    value_rows = cache_rows[1].astype(jnp.float32).reshape(window, KVH, HD)[:, head_map]
    scores = jnp.einsum('hd,whd->hw', heads, key_rows) * HD ** (-0.5)
    capped = softcap * jnp.tanh(scores / softcap)
    positions = jnp.arange(window).astype(jnp.int32)
    weights = jnp.where(positions[None, :] < live_length, jnp.exp(capped), jnp.float32(0.0))
    rounded = weights.astype(jnp.bfloat16).astype(jnp.float32)
    numerator = jnp.einsum('hw,whd->hd', rounded, value_rows)
    return (numerator, lax.optimization_barrier(jnp.sum(weights, axis=-1)))

def reference(hidden_input, queries, prompt_cache, suffix_cache, owner_replica, group_slot, prompt_length, suffix_length, output_weight, post_gain):
    head_map = (jnp.arange(QH) // (QH // KVH)).astype(jnp.int32)

    def attend_one(inputs):
        query_row, own_cache, owner_index, slot_index, own_length = inputs
        group_index = (owner_index * G_DEV + slot_index).astype(jnp.int32)
        shared = lax.dynamic_index_in_dim(prompt_cache, group_index, 0, keepdims=False)
        live_length = lax.dynamic_index_in_dim(prompt_length, group_index, 0, keepdims=False)
        heads = query_row.astype(jnp.float32).reshape(QH, HD)
        prompt_num, prompt_den = partial_attend(heads, shared, live_length, head_map)
        own_num, own_den = partial_attend(heads, own_cache, own_length, head_map)
        mixed = (prompt_num + own_num) / (prompt_den + own_den)[:, None]
        return mixed.reshape(QH * HD).astype(jnp.bfloat16)
    attention = lax.map(attend_one, (queries, suffix_cache, owner_replica[:, 0], group_slot, suffix_length))
    projected = jnp.dot(attention, output_weight, preferred_element_type=jnp.float32)
    mean_square = lax.optimization_barrier(jnp.mean(projected * projected, axis=-1, keepdims=True))
    normed = projected * lax.rsqrt(mean_square + epsilon) * post_gain[None, :]
    return (hidden_input.astype(jnp.float32) + normed).astype(jnp.bfloat16)
```

```python
import jax
import jax.numpy as jnp
from jax import lax
from jax.sharding import PartitionSpec as P

HD = 256
softcap = 50.0
epsilon = 1e-06


def capped_weights(scores, alive):
    capped = softcap * jnp.tanh(scores / softcap)
    return jnp.where(alive, jnp.exp(capped), 0.0)


def prompt_part(queries, member, prompt_cache, prompt_length):
    items = queries.shape[0]
    size = prompt_cache.shape[2]
    rows = queries.reshape(items * 2, HD)
    who = jnp.repeat(member, 2)
    length = jnp.zeros((items * 2,), jnp.int32)
    scores = jnp.zeros((items * 2, size), jnp.float32)
    for g in range(prompt_cache.shape[0]):
        part = jnp.einsum("md,pd->mp", rows, prompt_cache[g, 0], preferred_element_type=jnp.float32)
        scores = jnp.where((who == g)[:, None], part, scores)
        length = jnp.where(who == g, prompt_length[g], length)
    positions = lax.broadcasted_iota(jnp.int32, (1, size), 1)
    weights = capped_weights(scores * HD ** (-0.5), positions < length[:, None])
    rounded = weights.astype(jnp.bfloat16)
    numerator = jnp.zeros((items * 2, HD), jnp.float32)
    for g in range(prompt_cache.shape[0]):
        part = jnp.einsum("mp,pd->md", rounded, prompt_cache[g, 1], preferred_element_type=jnp.float32)
        numerator = jnp.where((who == g)[:, None], part, numerator)
    return numerator.reshape(items, 2, HD), jnp.sum(weights, axis=-1).reshape(items, 2)


def suffix_part(queries, cache_rows, length):
    items = queries.shape[0]
    rows = queries.reshape(items, 2, HD)
    scores = jnp.einsum("mqd,msd->mqs", rows, cache_rows[:, 0], preferred_element_type=jnp.float32)
    alive = lax.broadcasted_iota(jnp.int32, (1, 1, cache_rows.shape[2]), 2) < length[:, None, None]
    weights = capped_weights(scores * HD ** (-0.5), alive)
    numerator = jnp.einsum("mqs,msd->mqd", weights.astype(jnp.bfloat16), cache_rows[:, 1], preferred_element_type=jnp.float32)
    return numerator, jnp.sum(weights, axis=-1)


def shards(hidden_input, queries, prompt_cache, suffix_cache, owner_replica, group_slot, prompt_length, suffix_length, output_weight, post_gain):
    replicas = lax.axis_size("replica")
    requests = queries.shape[0]
    slots = replicas * 2
    target = owner_replica[:, 0]
    ids = jnp.arange(requests)
    earlier = (target[:, None] == target[None, :]) & (ids[None, :] < ids[:, None])
    position = target * 2 + jnp.sum(earlier.astype(jnp.int32), axis=1)
    matches = lax.broadcasted_iota(jnp.int32, (slots, requests), 0) == position[None, :]
    onehot = matches.astype(jnp.bfloat16)
    send_queries = jnp.dot(onehot, queries, preferred_element_type=jnp.float32).astype(jnp.bfloat16)
    send_group = jnp.max(jnp.where(matches, group_slot[None, :], -1), axis=1)
    extra = jnp.broadcast_to(send_group[:, None].astype(jnp.bfloat16), (slots, 128))
    message = jnp.concatenate([send_queries, extra], axis=1).reshape(replicas, 2, -1)
    got = lax.all_to_all(message, "replica", split_axis=0, concat_axis=0, tiled=True).reshape(slots, -1)
    own_num, own_den = suffix_part(queries, suffix_cache, suffix_length)
    member = got[:, 512].astype(jnp.int32)
    num, den = prompt_part(got[:, :512], member, prompt_cache, prompt_length)
    safe = jnp.where(den > 0.0, den, 1.0)
    mean = (num / safe[..., None]).reshape(slots, 512).astype(jnp.bfloat16)
    high = den.astype(jnp.bfloat16)
    low = (den - high.astype(jnp.float32)).astype(jnp.bfloat16)
    tail = jnp.concatenate([high, low, jnp.zeros((slots, 124), jnp.bfloat16)], axis=1)
    back = jnp.concatenate([mean, tail], axis=1).reshape(replicas, 2, -1)
    returned = lax.all_to_all(back, "replica", split_axis=0, concat_axis=0, tiled=True).reshape(slots, -1)
    mine = jnp.dot(onehot.T, returned, preferred_element_type=jnp.float32)
    prompt_den = mine[:, 512:514] + mine[:, 514:516]
    prompt_num = mine[:, :512].reshape(requests, 2, HD) * prompt_den[..., None]
    attention = ((prompt_num + own_num) / (prompt_den + own_den)[..., None]).reshape(requests, 512).astype(jnp.bfloat16)
    partial_proj = jnp.dot(attention, output_weight, preferred_element_type=jnp.float32)
    total = lax.psum_scatter(partial_proj, "tensor", scatter_dimension=1, tiled=True)
    squares = lax.psum(jnp.sum(total * total, axis=-1), "tensor")
    mean_square = squares / (total.shape[1] * lax.axis_size("tensor"))
    normed = total * lax.rsqrt(mean_square + epsilon)[:, None] * post_gain[None, :]
    return (hidden_input.astype(jnp.float32) + normed).astype(jnp.bfloat16)


def solution(mesh):
    in_specs = (
        P("replica", "tensor"), P("replica", "tensor"), P("replica", None, None, "tensor"), P("replica", None, None, "tensor"),
        P("replica", None), P("replica"), P("replica"), P("replica"), P("tensor", None), P("tensor"),
    )
    return jax.shard_map(shards, mesh=mesh, in_specs=in_specs, out_specs=P("replica", "tensor"), check_vma=False)
```

```python
import functools

import jax
import jax.numpy as jnp
from jax import lax
from jax.experimental import pallas as pl
from jax.experimental.pallas import tpu as pltpu
from jax.sharding import PartitionSpec as P

MESH = pl.DeviceIdType.MESH
HD = 256
ROWS = 16
SOFTCAP = 50.0
EPSILON = 1e-06
F32, BF16 = jnp.float32, jnp.bfloat16


def capped_exp(scores):
    return jnp.exp(SOFTCAP * jnp.tanh(scores * (HD ** -0.5 / SOFTCAP)))


def nt(a, b):
    return lax.dot_general(a, b, (((1,), (1,)), ((), ())), preferred_element_type=F32)


def dot(a, b):
    return jnp.dot(a, b, preferred_element_type=F32)


def column(row, eye):
    return jnp.sum(jnp.where(eye, row, 0.0), axis=1, keepdims=True)


def kernel(
    R, T, M, width,
    owner_ref, slot_ref, slen_ref, plen_ref, gain_ref, q_ref, hidden_hbm, prompt_hbm, suffix_hbm, w_hbm,
    out_ref,
    kv, sfx, wv, hid, send, recv, back, ret, stage, qf, lenb, qsel, wts, num_s, den_s, psend, precv, sqsend, sqrecv,
    load_sem, ssem, rsem, bsem, tsem, psem, prsem, qsem, qrsem,
):
    me, t = lax.axis_index("replica"), lax.axis_index("tensor")
    G, _, size, _ = kv.shape
    S = sfx.shape[2]

    loads = [pltpu.make_async_copy(suffix_hbm, sfx, load_sem.at[0])]
    for c in range(2):
        for g in range(G):
            loads.append(pltpu.make_async_copy(prompt_hbm.at[g, c], kv.at[g, c], load_sem.at[1 + c * G + g]))
    loads.append(pltpu.make_async_copy(w_hbm, wv, load_sem.at[1 + 2 * G]))
    loads.append(pltpu.make_async_copy(hidden_hbm, hid, load_sem.at[2 + 2 * G]))
    for load in loads:
        load.start()

    barrier = pltpu.get_barrier_semaphore()

    def greet(off, carry):
        pl.semaphore_signal(barrier, inc=1, device_id=(lax.rem(me + off, R), t), device_id_type=MESH)
        return carry

    lax.fori_loop(1, R, greet, 0)
    for off in range(1, T):
        pl.semaphore_signal(barrier, inc=1, device_id=(me, lax.rem(t + off, T)), device_id_type=MESH)

    sub = lax.broadcasted_iota(jnp.int32, (M, M), 0)
    lane = lax.broadcasted_iota(jnp.int32, (M, M), 1)
    eye = sub == lane
    o_row = owner_ref[...].astype(F32)
    o_col = column(o_row, eye)
    same = jnp.where(o_row == o_col, 1.0, 0.0)
    rank_row = jnp.sum(jnp.where(sub < lane, same, 0.0), axis=0, keepdims=True)
    rank_col = jnp.sum(jnp.where(lane < sub, same, 0.0), axis=1, keepdims=True)
    owner_id = lax.broadcasted_iota(jnp.int32, (R, M), 0).astype(F32)
    at_owner = owner_id == o_row
    member = slot_ref[...].astype(F32) + 1.0
    queries = q_ref[...]
    for k in range(2):
        pick = jnp.where(at_owner & (rank_row == float(k)), 1.0, 0.0)
        rows = dot(pick.astype(BF16), queries)
        for c in range(4):
            stage[pl.ds(k * 4 + c, R, stride=ROWS), :] = rows[:, c * 128:(c + 1) * 128]
        gid = jnp.sum(pick * member, axis=1, keepdims=True) - 1.0
        stage[pl.ds(8 + k, R, stride=ROWS), :] = jnp.broadcast_to(gid, (R, 128))
    for j in range(10, ROWS):
        stage[pl.ds(j, R, stride=ROWS), :] = jnp.zeros((R, 128), F32)
    send[...] = stage[...].astype(BF16).reshape(R, ROWS, 128)

    pl.semaphore_wait(barrier, R - 1 + T - 1)

    def exchange(src, dst, send_sem, recv_sem):
        def go(off, carry):
            to = lax.rem(me + off, R)
            pltpu.make_async_remote_copy(
                src_ref=src.at[to], dst_ref=dst.at[me], send_sem=send_sem, recv_sem=recv_sem,
                device_id=(to, t), device_id_type=MESH,
            ).start()
            return carry

        lax.fori_loop(1, R, go, 0)
        pltpu.make_async_copy(src.at[me], dst.at[me], recv_sem).start()

    def arrived(dst, recv_sem):
        pltpu.make_async_copy(dst, dst, recv_sem).wait()

    def departed(src, send_sem):
        part = src.at[pl.ds(0, R - 1)]
        pltpu.make_async_copy(part, part, send_sem).wait()

    exchange(send, recv, ssem, rsem)

    qf[...] = queries.astype(F32)
    lenb[...] = jnp.broadcast_to(column(slen_ref[...].astype(F32), eye), lenb.shape)
    loads[0].wait()
    row8 = lax.rem(lax.broadcasted_iota(jnp.int32, (16, 8 * S), 0), 8)
    lanes = lax.broadcasted_iota(jnp.int32, (16, 8 * S), 1)
    own_row = lanes // S == row8
    place = lax.rem(lanes, S).astype(F32)
    for b in range(M // 8):
        q8 = qf[8 * b:8 * b + 8, :]
        both = jnp.concatenate([q8[:, :HD], q8[:, HD:]], axis=0).astype(BF16)
        length = lenb[8 * b:8 * b + 8, :]
        length = jnp.concatenate([length, length], axis=0)
        keys = sfx[8 * b:8 * b + 8, 0].reshape(8 * S, HD)
        values = sfx[8 * b:8 * b + 8, 1].reshape(8 * S, HD)
        weights = jnp.where(own_row & (place < length), capped_exp(nt(both, keys)), 0.0)
        den = jnp.sum(weights, axis=1, keepdims=True)
        num = dot(weights.astype(BF16), values)
        for h in range(2):
            num_s[8 * b:8 * b + 8, h * HD:(h + 1) * HD] = num[8 * h:8 * h + 8, :]
            den_s[8 * b:8 * b + 8, h * HD:(h + 1) * HD] = jnp.broadcast_to(den[8 * h:8 * h + 8, :], (8, HD))

    arrived(recv, rsem)
    stage[...] = recv[...].reshape(R * ROWS, 128).astype(F32)

    def chunk(j):
        return stage[pl.ds(j, R, stride=ROWS), :]

    rows = jnp.concatenate(
        [jnp.concatenate([chunk(k * 4 + 2 * h), chunk(k * 4 + 2 * h + 1)], axis=1) for k in range(2) for h in range(2)], axis=0
    )
    gid = jnp.concatenate([chunk(8), chunk(8), chunk(9), chunk(9)], axis=0)
    gid2 = jnp.concatenate([gid, gid], axis=1)
    length = jnp.zeros(gid.shape, jnp.int32)
    for g in range(G):
        qsel[g] = jnp.where(gid2 == float(g), rows, 0.0).astype(BF16)
        length = jnp.where(gid == float(g), plen_ref[0, g], length)
    for load in loads[1:1 + G]:
        load.wait()
    CH = 512
    length4 = jnp.concatenate([length] * (CH // 128), axis=1)
    total_den = jnp.zeros((4 * R, 1), F32)
    for p in range(size // CH):
        scores = nt(qsel[0], kv[0, 0, p * CH:(p + 1) * CH, :])
        for g in range(1, G):
            scores = scores + nt(qsel[g], kv[g, 0, p * CH:(p + 1) * CH, :])
        position = lax.broadcasted_iota(jnp.int32, scores.shape, 1) + p * CH
        weights = jnp.where(position < length4, capped_exp(scores), 0.0)
        total_den = total_den + jnp.sum(weights, axis=1, keepdims=True)
        wts[:, p * CH:(p + 1) * CH] = weights.astype(BF16)
    for load in loads[1 + G:1 + 2 * G]:
        load.wait()
    num = jnp.zeros((4 * R, HD), F32)
    for g in range(G):
        num = jnp.where(gid2 == float(g), dot(wts[...], kv[g, 1]), num)
    mean = num / jnp.where(total_den > 0.0, total_den, 1.0)
    high = total_den.astype(BF16).astype(F32)
    low = total_den - high
    for k in range(2):
        for h in range(2):
            part = slice((k * 2 + h) * R, (k * 2 + h + 1) * R)
            stage[pl.ds(k * 4 + 2 * h, R, stride=ROWS), :] = mean[part, :128]
            stage[pl.ds(k * 4 + 2 * h + 1, R, stride=ROWS), :] = mean[part, 128:]
            stage[pl.ds(8 + k * 2 + h, R, stride=ROWS), :] = jnp.broadcast_to(high[part], (R, 128))
            stage[pl.ds(12 + k * 2 + h, R, stride=ROWS), :] = jnp.broadcast_to(low[part], (R, 128))
    back[...] = stage[...].astype(BF16).reshape(R, ROWS, 128)
    exchange(back, ret, bsem, tsem)

    spot = lax.broadcasted_iota(jnp.int32, (M, 2 * R), 1).astype(F32)
    fetch = jnp.where(spot == rank_col * float(R) + o_col, 1.0, 0.0).astype(BF16)
    arrived(ret, tsem)
    stage[...] = ret[...].reshape(R * ROWS, 128).astype(F32)
    table = jnp.concatenate(
        [
            jnp.concatenate([chunk(j) for j in (k * 4, k * 4 + 1, k * 4 + 2, k * 4 + 3, 8 + k * 2, 9 + k * 2, 12 + k * 2, 13 + k * 2)], axis=1)
            for k in range(2)
        ],
        axis=0,
    ).astype(BF16)
    mine = dot(fetch, table)
    den_p = [mine[:, 512 + 128 * h:640 + 128 * h] + mine[:, 768 + 128 * h:896 + 128 * h] for h in range(2)]
    den_p = jnp.concatenate([den_p[0], den_p[0], den_p[1], den_p[1]], axis=1)
    attention = ((mine[:, :512] * den_p + num_s[...]) / (den_p + den_s[...])).astype(BF16)

    loads[1 + 2 * G].wait()

    def projected(which):
        return dot(attention, wv[:, pl.ds(pl.multiple_of(which * width, 128), width)])

    copies = []
    for off in (2, 1, 3):
        to = lax.rem(t + off, T)
        psend[off] = projected(to).astype(BF16)
        copies.append(pltpu.make_async_remote_copy(
            src_ref=psend.at[off], dst_ref=precv.at[off], send_sem=psem.at[off], recv_sem=prsem.at[off],
            device_id=(me, to), device_id_type=MESH,
        ))
        copies[-1].start()
    total = projected(t)
    for copy in copies:
        copy.wait_recv()
    for off in range(1, T):
        total = total + precv[off].astype(F32)
    square = jnp.sum(total * total, axis=1, keepdims=True)
    eye_wide = lax.broadcasted_iota(jnp.int32, (M, 128), 0) == lax.broadcasted_iota(jnp.int32, (M, 128), 1)
    square_row = jnp.sum(jnp.where(eye_wide, square, 0.0), axis=0, keepdims=True)
    sqsend[...] = jnp.broadcast_to(square_row, (8, 128))
    squares = []
    for off in (2, 1, 3):
        squares.append(pltpu.make_async_remote_copy(
            src_ref=sqsend, dst_ref=sqrecv.at[off], send_sem=qsem.at[off], recv_sem=qrsem.at[off],
            device_id=(me, lax.rem(t + off, T)), device_id_type=MESH,
        ))
        squares[-1].start()
    loads[2 + 2 * G].wait()
    for copy in squares:
        copy.wait_recv()
    for off in range(1, T):
        square_row = square_row + sqrecv[off, 0:1, :]
    mean_square = column(square_row, eye_wide) * (1.0 / (width * T))
    normed = total * lax.rsqrt(mean_square + EPSILON) * gain_ref[...]
    out_ref[...] = (hid[...].astype(F32) + normed).astype(BF16)

    departed(send, ssem)
    departed(back, bsem)
    for copy in copies + squares:
        copy.wait_send()


def shards(
    hidden_input, queries, prompt_cache, suffix_cache, owner_replica, group_slot, prompt_length, suffix_length,
    output_weight, post_gain,
):
    R, T = lax.axis_size("replica"), lax.axis_size("tensor")
    M, width = hidden_input.shape
    G, _, size, _ = prompt_cache.shape
    S = suffix_cache.shape[2]
    vmem = pl.BlockSpec(memory_space=pltpu.VMEM)
    hbm = pl.BlockSpec(memory_space=pl.ANY)
    smem = pl.BlockSpec(memory_space=pltpu.SMEM)
    dma = pltpu.SemaphoreType.DMA
    message = pltpu.VMEM((R, ROWS, 128), BF16)
    return pl.pallas_call(
        functools.partial(kernel, R, T, M, width),
        out_shape=jax.ShapeDtypeStruct((M, width), BF16),
        in_specs=[vmem, vmem, vmem, smem, vmem, vmem, hbm, hbm, hbm, hbm],
        out_specs=vmem,
        scratch_shapes=[
            pltpu.VMEM(prompt_cache.shape, BF16),
            pltpu.VMEM(suffix_cache.shape, BF16),
            pltpu.VMEM(output_weight.shape, BF16),
            pltpu.VMEM((M, width), BF16),
            message, message, message, message,
            pltpu.VMEM((R * ROWS, 128), F32),
            pltpu.VMEM((M, 2 * HD), F32),
            pltpu.VMEM((M, 8 * S), F32),
            pltpu.VMEM((G, 4 * R, HD), BF16),
            pltpu.VMEM((4 * R, size), BF16),
            pltpu.VMEM((M, 2 * HD), F32),
            pltpu.VMEM((M, 2 * HD), F32),
            pltpu.VMEM((T, M, width), BF16),
            pltpu.VMEM((T, M, width), BF16),
            pltpu.VMEM((8, 128), F32),
            pltpu.VMEM((T, 8, 128), F32),
            dma((3 + 2 * G,)), dma(()), dma(()), dma(()), dma(()), dma((T,)), dma((T,)), dma((T,)), dma((T,)),
        ],
        compiler_params=pltpu.CompilerParams(collective_id=0, has_side_effects=True, vmem_limit_bytes=56 * 2 ** 20),
        name="decode_attention",
    )(
        owner_replica.reshape(1, M), group_slot.reshape(1, M), suffix_length.reshape(1, M), prompt_length.reshape(1, G),
        post_gain.reshape(1, width), queries, hidden_input, prompt_cache, suffix_cache, output_weight,
    )


def solution(mesh):
    in_specs = (
        P("replica", "tensor"), P("replica", "tensor"), P("replica", None, None, "tensor"), P("replica", None, None, "tensor"),
        P("replica", None), P("replica"), P("replica"), P("replica"), P("tensor", None), P("tensor"),
    )
    return jax.shard_map(shards, mesh=mesh, in_specs=in_specs, out_specs=P("replica", "tensor"), check_vma=False)
```

```python
import functools

import jax
import jax.numpy as jnp
from jax import lax
from jax.experimental import pallas as pl
from jax.experimental.pallas import tpu as pltpu
from jax.sharding import PartitionSpec as P

MESH = pl.DeviceIdType.MESH
HD = 256
ROWS = 16
LIVE = 10
SOFTCAP = 50.0
EPSILON = 1e-06
F32, BF16 = jnp.float32, jnp.bfloat16


def capped_exp(scores):
    return jnp.exp(SOFTCAP * jnp.tanh(scores * (HD ** -0.5 / SOFTCAP)))


def nt(a, b):
    return lax.dot_general(a, b, (((1,), (1,)), ((), ())), preferred_element_type=F32)


def dot(a, b):
    return jnp.dot(a, b, preferred_element_type=F32)


def column(row, eye):
    return jnp.sum(jnp.where(eye, row, 0.0), axis=1, keepdims=True)


def grid_of(R):
    return (R // 8, 4, 2) if R >= 64 else (R // 2, 1, 2)


def hops(off, dims):
    return sum(min(o, n - o) * w for o, n, w in zip(off, dims, (1.0, 1.0, 0.5)))


def kernel(
    R, T, M, width,
    owner_hbm, slot_hbm, slen_hbm, plen_hbm, gain_hbm, q_hbm, hidden_hbm, prompt_hbm, suffix_hbm, w_hbm,
    out_ref,
    owner_ref, slot_ref, slen_ref, plen_ref, gain_ref, q_ref,
    kv, sfx, wv, hid, send, recv, back, ret, stage, stage_out, qf, lenb, qsel, wts, num_s, den_s,
    farsend, farrecv, dirsend, dirrecv, sumsend, sumrecv, sqsend, sqrecv,
    small_sem, load_sem, ssem, rsem, bsem, tsem, psem, prsem, qsem, qrsem,
):
    me, t = lax.axis_index("replica"), lax.axis_index("tensor")
    G, _, size, _ = kv.shape
    S = sfx.shape[2]
    NZ, NX, NC = dims = grid_of(R)
    H = R // 2

    smalls = [
        pltpu.make_async_copy(src, dst, small_sem.at[n])
        for n, (src, dst) in enumerate((
            (owner_hbm, owner_ref), (slot_hbm, slot_ref), (q_hbm, q_ref), (slen_hbm, slen_ref), (plen_hbm, plen_ref), (gain_hbm, gain_ref),
        ))
    ]
    for load in smalls:
        load.start()

    z, x, c = me // (NX * NC), lax.rem(me // NC, NX), lax.rem(me, NC)
    ahead = [[lax.rem(p + o, n) for o in range(n)] for p, n in ((z, NZ), (x, NX), (c, NC))]
    behind = [[lax.rem(p + n - o, n) for o in range(n)] for p, n in ((z, NZ), (x, NX), (c, NC))]
    offsets = [(lax_z, lax_x, lax_c) for lax_z in range(NZ) for lax_x in range(NX) for lax_c in range(NC)]
    offsets = sorted(offsets, key=lambda off: -hops(off, dims))[:-1]

    def index_of(off):
        return ((off[0] + NZ - NZ // 4) % NZ) * NX * NC + off[1] * NC + off[2]

    def device(table, off):
        return table[0][off[0]] * (NX * NC) + table[1][off[1]] * NC + table[2][off[2]]

    own = index_of((0, 0, 0))

    barrier = pltpu.get_barrier_semaphore()
    for off in offsets:
        pl.semaphore_signal(barrier, inc=1, device_id=(device(ahead, off), t), device_id_type=MESH)
    for off in range(1, T):
        pl.semaphore_signal(barrier, inc=1, device_id=(me, lax.rem(t + off, T)), device_id_type=MESH)

    loads = [pltpu.make_async_copy(suffix_hbm, sfx, load_sem.at[0])]
    for a in range(2):
        for g in range(G):
            loads.append(pltpu.make_async_copy(prompt_hbm.at[g, a], kv.at[g, a], load_sem.at[1 + a * G + g]))
    loads.append(pltpu.make_async_copy(w_hbm, wv, load_sem.at[1 + 2 * G]))
    loads.append(pltpu.make_async_copy(hidden_hbm, hid, load_sem.at[2 + 2 * G]))
    for load in loads:
        load.start()

    sub = lax.broadcasted_iota(jnp.int32, (M, M), 0)
    lane = lax.broadcasted_iota(jnp.int32, (M, M), 1)
    eye = sub == lane

    def place_of(owner):
        oz, rest = owner // (NX * NC), lax.rem(owner, NX * NC)
        dz = lax.rem(oz - z + 2 * NZ - NZ // 4, NZ)
        dx = lax.rem(rest // NC - x + NX, NX)
        dc = lax.rem(lax.rem(rest, NC) - c + NC, NC)
        return dz * (NX * NC) + dx * NC + dc

    for load in smalls[:3]:
        load.wait()
    o_row = place_of(owner_ref[...]).astype(F32)
    o_col = column(o_row, eye)
    same = jnp.where(o_row == o_col, 1.0, 0.0)
    rank_row = jnp.sum(jnp.where(sub < lane, same, 0.0), axis=0, keepdims=True)
    rank_col = jnp.sum(jnp.where(lane < sub, same, 0.0), axis=1, keepdims=True)
    owner_id = lax.broadcasted_iota(jnp.int32, (R, M), 0).astype(F32)
    at_owner = owner_id == o_row
    member = slot_ref[...].astype(F32) + 1.0
    queries = q_ref[...]
    for k in range(2):
        pick = jnp.where(at_owner & (rank_row == float(k)), 1.0, 0.0)
        rows = dot(pick.astype(BF16), queries)
        for n in range(4):
            stage[pl.ds(k * 4 + n, R, stride=ROWS), :] = rows[:, n * 128:(n + 1) * 128]
        gid = jnp.sum(pick * member, axis=1, keepdims=True) - 1.0
        stage[pl.ds(8 + k, R, stride=ROWS), :] = jnp.broadcast_to(gid, (R, 128))
    send[...] = stage[...].astype(BF16).reshape(R, ROWS, 128)

    pl.semaphore_wait(barrier, R - 1 + T - 1)

    live = pl.ds(0, LIVE)

    def dispatch(src, dst, send_sem, recv_sem, table, low, high):
        for off in offsets:
            n = index_of(off)
            if low <= n < high:
                pltpu.make_async_remote_copy(
                    src_ref=src.at[n, live], dst_ref=dst.at[n, live], send_sem=send_sem, recv_sem=recv_sem,
                    device_id=(device(table, off), t), device_id_type=MESH,
                ).start()
        if low <= own < high:
            pltpu.make_async_copy(src.at[own, live], dst.at[own, live], recv_sem).start()

    def arrived(dst, recv_sem):
        part = dst.at[pl.ds(0, R), live]
        pltpu.make_async_copy(part, part, recv_sem).wait()

    def departed(src, send_sem):
        part = src.at[pl.ds(0, R - 1), live]
        pltpu.make_async_copy(part, part, send_sem).wait()

    dispatch(send, recv, ssem, rsem, ahead, 0, R)

    for load in smalls[3:]:
        load.wait()
    qf[...] = queries.astype(F32)
    lenb[...] = jnp.broadcast_to(column(slen_ref[...].astype(F32), eye), lenb.shape)
    loads[0].wait()
    row8 = lax.rem(lax.broadcasted_iota(jnp.int32, (16, 8 * S), 0), 8)
    lanes = lax.broadcasted_iota(jnp.int32, (16, 8 * S), 1)
    own_row = lanes // S == row8
    place = lax.rem(lanes, S).astype(F32)
    for b in range(M // 8):
        q8 = qf[8 * b:8 * b + 8, :]
        both = jnp.concatenate([q8[:, :HD], q8[:, HD:]], axis=0).astype(BF16)
        length = lenb[8 * b:8 * b + 8, :]
        length = jnp.concatenate([length, length], axis=0)
        keys = sfx[8 * b:8 * b + 8, 0].reshape(8 * S, HD)
        values = sfx[8 * b:8 * b + 8, 1].reshape(8 * S, HD)
        weights = jnp.where(own_row & (place < length), capped_exp(nt(both, keys)), 0.0)
        den = jnp.sum(weights, axis=1, keepdims=True)
        num = dot(weights.astype(BF16), values)
        for h in range(2):
            num_s[8 * b:8 * b + 8, h * HD:(h + 1) * HD] = num[8 * h:8 * h + 8, :]
            den_s[8 * b:8 * b + 8, h * HD:(h + 1) * HD] = jnp.broadcast_to(den[8 * h:8 * h + 8, :], (8, HD))
    for load in loads[1:1 + 2 * G]:
        load.wait()

    arrived(recv, rsem)
    stage[...] = recv[...].reshape(R * ROWS, 128).astype(F32)
    CH = 512
    quarter = lax.broadcasted_iota(jnp.int32, (H, 128), 1) // 32
    for half in range(2):
        first = half * H

        def chunk(n):
            return stage[pl.ds(first * ROWS + n, H, stride=ROWS), :]

        rows = jnp.concatenate(
            [jnp.concatenate([chunk(k * 4 + 2 * h), chunk(k * 4 + 2 * h + 1)], axis=1) for k in range(2) for h in range(2)], axis=0
        )
        gid = jnp.concatenate([chunk(8), chunk(8), chunk(9), chunk(9)], axis=0)
        gid2 = jnp.concatenate([gid, gid], axis=1)
        length = jnp.zeros(gid.shape, jnp.int32)
        for g in range(G):
            qsel[half, g] = jnp.where(gid2 == float(g), rows, 0.0).astype(BF16)
            length = jnp.where(gid == float(g), plen_ref[0:1, g:g + 1], length)
        length4 = jnp.concatenate([length] * (CH // 128), axis=1)
        total_den = jnp.zeros((4 * H, 1), F32)
        for p in range(size // CH):
            scores = nt(qsel[half, 0], kv[0, 0, p * CH:(p + 1) * CH, :])
            for g in range(1, G):
                scores = scores + nt(qsel[half, g], kv[g, 0, p * CH:(p + 1) * CH, :])
            position = lax.broadcasted_iota(jnp.int32, scores.shape, 1) + p * CH
            weights = jnp.where(position < length4, capped_exp(scores), 0.0)
            total_den = total_den + jnp.sum(weights, axis=1, keepdims=True)
            wts[half, :, p * CH:(p + 1) * CH] = weights.astype(BF16)
        num = jnp.zeros((4 * H, HD), F32)
        for g in range(G):
            num = jnp.where(gid2 == float(g), dot(wts[half], kv[g, 1]), num)
        mean = num / jnp.where(total_den > 0.0, total_den, 1.0)
        high = total_den.astype(BF16).astype(F32)
        low = total_den - high
        for k in range(2):
            dens = jnp.zeros((H, 128), F32)
            for h in range(2):
                part = slice((k * 2 + h) * H, (k * 2 + h + 1) * H)
                stage_out[pl.ds(first * ROWS + k * 4 + 2 * h, H, stride=ROWS), :] = mean[part, :128]
                stage_out[pl.ds(first * ROWS + k * 4 + 2 * h + 1, H, stride=ROWS), :] = mean[part, 128:]
                dens = jnp.where(quarter == 2 * h, high[part], jnp.where(quarter == 2 * h + 1, low[part], dens))
            stage_out[pl.ds(first * ROWS + 8 + k, H, stride=ROWS), :] = dens
        back[first:first + H] = stage_out[first * ROWS:(first + H) * ROWS, :].astype(BF16).reshape(H, ROWS, 128)
        dispatch(back, ret, bsem, tsem, behind, first, first + H)

    spot = lax.broadcasted_iota(jnp.int32, (M, 2 * R), 1).astype(F32)
    fetch = jnp.where(spot == rank_col * float(R) + o_col, 1.0, 0.0).astype(BF16)
    loads[1 + 2 * G].wait()
    loads[2 + 2 * G].wait()
    arrived(ret, tsem)
    stage[...] = ret[...].reshape(R * ROWS, 128).astype(F32)

    def answers(n):
        return stage[pl.ds(n, R, stride=ROWS), :]

    table = jnp.concatenate(
        [jnp.concatenate([answers(n) for n in (k * 4, k * 4 + 1, k * 4 + 2, k * 4 + 3, 8 + k)], axis=1) for k in range(2)], axis=0
    ).astype(BF16)
    mine = dot(fetch, table)
    parts = []
    for h in range(2):
        den_p = mine[:, 512 + 64 * h:513 + 64 * h] + mine[:, 544 + 64 * h:545 + 64 * h]
        cols = slice(h * HD, (h + 1) * HD)
        parts.append((mine[:, cols] * den_p + num_s[:, cols]) / (den_p + den_s[:, cols]))
    attention = jnp.concatenate(parts, axis=1).astype(BF16)

    def projected(which):
        return dot(attention, wv[:, pl.ds(pl.multiple_of(which * width, 128), width)])

    half_rows = M // 2
    right, left = lax.rem(t + 1, T), lax.rem(t + T - 1, T)

    def hand_on(n, src, dst, to):
        copy = pltpu.make_async_remote_copy(
            src_ref=src, dst_ref=dst, send_sem=psem.at[n], recv_sem=prsem.at[n], device_id=(me, to), device_id_type=MESH,
        )
        copy.start()
        return copy

    far = projected(lax.rem(t + 2, T)).astype(BF16)
    farsend[0], farsend[1] = far[:half_rows], far[half_rows:]
    far_right = hand_on(0, farsend.at[0], farrecv.at[0], right)
    far_left = hand_on(1, farsend.at[1], farrecv.at[1], left)
    to_right, to_left = projected(right), projected(left)
    dirsend[0] = to_left[:half_rows].astype(BF16)
    dirsend[1] = to_right[half_rows:].astype(BF16)
    direct_left = hand_on(2, dirsend.at[0], dirrecv.at[0], left)
    direct_right = hand_on(3, dirsend.at[1], dirrecv.at[1], right)
    total = projected(t)
    far_right.wait_recv()
    sumsend[0] = (to_right[:half_rows] + farrecv[0].astype(F32)).astype(BF16)
    sum_right = hand_on(4, sumsend.at[0], sumrecv.at[0], right)
    far_left.wait_recv()
    sumsend[1] = (to_left[half_rows:] + farrecv[1].astype(F32)).astype(BF16)
    sum_left = hand_on(5, sumsend.at[1], sumrecv.at[1], left)
    for copy in (direct_left, direct_right, sum_right, sum_left):
        copy.wait_recv()
    total = total + jnp.concatenate([dirrecv[n].astype(F32) + sumrecv[n].astype(F32) for n in range(2)], axis=0)

    square = jnp.sum(total * total, axis=1, keepdims=True)
    eye_wide = lax.broadcasted_iota(jnp.int32, (M, 128), 0) == lax.broadcasted_iota(jnp.int32, (M, 128), 1)
    square_row = jnp.sum(jnp.where(eye_wide, square, 0.0), axis=0, keepdims=True)
    sqsend[...] = jnp.broadcast_to(square_row, (8, 128))
    squares = []
    for off in (2, 1, 3):
        squares.append(pltpu.make_async_remote_copy(
            src_ref=sqsend, dst_ref=sqrecv.at[off], send_sem=qsem.at[off], recv_sem=qrsem.at[off],
            device_id=(me, lax.rem(t + off, T)), device_id_type=MESH,
        ))
        squares[-1].start()
    scaled = total * gain_ref[...].reshape(1, width)
    departed(send, ssem)
    departed(back, bsem)
    for copy in squares:
        copy.wait_recv()
    for off in range(1, T):
        square_row = square_row + sqrecv[off, 0:1, :]
    mean_square = column(square_row, eye_wide) * (1.0 / (width * T))
    out_ref[...] = (hid[...].astype(F32) + scaled * lax.rsqrt(mean_square + EPSILON)).astype(BF16)

    for copy in (far_right, far_left, direct_left, direct_right, sum_right, sum_left, *squares):
        copy.wait_send()


def shards(
    hidden_input, queries, prompt_cache, suffix_cache, owner_replica, group_slot, prompt_length, suffix_length,
    output_weight, post_gain,
):
    R, T = lax.axis_size("replica"), lax.axis_size("tensor")
    M, width = hidden_input.shape
    G, _, size, _ = prompt_cache.shape
    S = suffix_cache.shape[2]
    vmem = pl.BlockSpec(memory_space=pltpu.VMEM)
    hbm = pl.BlockSpec(memory_space=pl.ANY)
    dma = pltpu.SemaphoreType.DMA
    message = pltpu.VMEM((R, ROWS, 128), BF16)
    return pl.pallas_call(
        functools.partial(kernel, R, T, M, width),
        out_shape=jax.ShapeDtypeStruct((M, width), BF16),
        in_specs=[hbm] * 10,
        out_specs=vmem,
        scratch_shapes=[
            pltpu.VMEM((1, M), jnp.int32), pltpu.VMEM((1, M), jnp.int32), pltpu.VMEM((1, M), jnp.int32), pltpu.VMEM((1, G), jnp.int32),
            pltpu.VMEM((width,), F32), pltpu.VMEM(queries.shape, BF16),
            pltpu.VMEM(prompt_cache.shape, BF16),
            pltpu.VMEM(suffix_cache.shape, BF16),
            pltpu.VMEM(output_weight.shape, BF16),
            pltpu.VMEM((M, width), BF16),
            message, message, message, message,
            pltpu.VMEM((R * ROWS, 128), F32),
            pltpu.VMEM((R * ROWS, 128), F32),
            pltpu.VMEM((M, 2 * HD), F32),
            pltpu.VMEM((M, 8 * S), F32),
            pltpu.VMEM((2, G, 2 * R, HD), BF16),
            pltpu.VMEM((2, 2 * R, size), BF16),
            pltpu.VMEM((M, 2 * HD), F32),
            pltpu.VMEM((M, 2 * HD), F32),
            *[pltpu.VMEM((2, M // 2, width), BF16)] * 6,
            pltpu.VMEM((8, 128), F32),
            pltpu.VMEM((T, 8, 128), F32),
            dma((6,)), dma((3 + 2 * G,)), dma(()), dma(()), dma(()), dma(()), dma((6,)), dma((6,)), dma((T,)), dma((T,)),
        ],
        compiler_params=pltpu.CompilerParams(collective_id=0, has_side_effects=True, vmem_limit_bytes=56 * 2 ** 20),
        name="decode_attention",
    )(
        owner_replica.reshape(1, M), group_slot.reshape(1, M), suffix_length.reshape(1, M), prompt_length.reshape(1, G),
        post_gain, queries, hidden_input, prompt_cache, suffix_cache, output_weight,
    )


def solution(mesh):
    in_specs = (
        P("replica", "tensor"), P("replica", "tensor"), P("replica", None, None, "tensor"), P("replica", None, None, "tensor"),
        P("replica", None), P("replica"), P("replica"), P("replica"), P("tensor", None), P("tensor"),
    )
    return jax.shard_map(shards, mesh=mesh, in_specs=in_specs, out_specs=P("replica", "tensor"), check_vma=False)
```

```python
import functools

import jax
import jax.numpy as jnp
from jax import lax
from jax.experimental import pallas as pl
from jax.experimental.pallas import tpu as pltpu
from jax.sharding import PartitionSpec as P

MESH = pl.DeviceIdType.MESH
HD = 256
PARTS = 2
ROWS = 16
LIVE = 10
SOFTCAP = 50.0
EPSILON = 1e-06
F32, BF16 = jnp.float32, jnp.bfloat16


def capped_exp(scores):
    return jnp.exp(SOFTCAP * jnp.tanh(scores * (HD ** -0.5 / SOFTCAP)))


def nt(a, b):
    return lax.dot_general(a, b, (((1,), (1,)), ((), ())), preferred_element_type=F32)


def dot(a, b):
    return jnp.dot(a, b, preferred_element_type=F32)


def column(row, eye):
    return jnp.sum(jnp.where(eye, row, 0.0), axis=1, keepdims=True)


def grid_of(R):
    return (R // 8, 4, 2) if R >= 64 else (R // 2, 1, 2)


def hops(off, dims):
    return sum(min(o, n - o) * w for o, n, w in zip(off, dims, (1.0, 1.0, 0.5)))


def kernel(
    R, T, M, width,
    owner_hbm, slot_hbm, slen_hbm, plen_hbm, gain_hbm, q_hbm, hidden_hbm, prompt_hbm, suffix_hbm, w_hbm,
    out_ref,
    owner_ref, slot_ref, slen_ref, plen_ref, gain_ref, q_ref,
    kv, sfx, wcol, hid, send, recv, back, ret, stage, stage_out, qf, lenb, qsel, wts, num_s, den_s,
    atts, far, sqsend, sqrecv,
    small_sem, load_sem, ssem, rsem, bsem, tsem, psem, prsem, wsem, wrsem, fsem, frsem, qsem, qrsem,
):
    me, t = lax.axis_index("replica"), lax.axis_index("tensor")
    G, _, size, _ = kv.shape
    S = sfx.shape[2]
    NZ, NX, NC = dims = grid_of(R)
    H = R // PARTS

    smalls = [
        pltpu.make_async_copy(src, dst, small_sem.at[n])
        for n, (src, dst) in enumerate((
            (owner_hbm, owner_ref), (slot_hbm, slot_ref), (q_hbm, q_ref), (slen_hbm, slen_ref), (plen_hbm, plen_ref), (gain_hbm, gain_ref),
        ))
    ]
    for load in smalls:
        load.start()

    z, x, c = me // (NX * NC), lax.rem(me // NC, NX), lax.rem(me, NC)
    ahead = [[lax.rem(p + o, n) for o in range(n)] for p, n in ((z, NZ), (x, NX), (c, NC))]
    behind = [[lax.rem(p + n - o, n) for o in range(n)] for p, n in ((z, NZ), (x, NX), (c, NC))]
    offsets = [(lax_z, lax_x, lax_c) for lax_z in range(NZ) for lax_x in range(NX) for lax_c in range(NC)]
    offsets = sorted(offsets, key=lambda off: -hops(off, dims))[:-1]

    def index_of(off):
        return ((off[0] + NZ - NZ // 4) % NZ) * NX * NC + off[1] * NC + off[2]

    def device(table, off):
        return table[0][off[0]] * (NX * NC) + table[1][off[1]] * NC + table[2][off[2]]

    own = index_of((0, 0, 0))

    barrier = pltpu.get_barrier_semaphore()
    for off in offsets:
        pl.semaphore_signal(barrier, inc=1, device_id=(device(ahead, off), t), device_id_type=MESH)
    for off in range(1, T):
        pl.semaphore_signal(barrier, inc=1, device_id=(me, lax.rem(t + off, T)), device_id_type=MESH)

    loads = [pltpu.make_async_copy(suffix_hbm, sfx, load_sem.at[0])]
    for a in range(2):
        for g in range(G):
            loads.append(pltpu.make_async_copy(prompt_hbm.at[g, a], kv.at[g, a], load_sem.at[1 + a * G + g]))
    def columns(which):
        return pl.ds(pl.multiple_of(which * width, 128), width)

    loads.append(pltpu.make_async_copy(w_hbm.at[:, columns(t)], wcol.at[0], load_sem.at[1 + 2 * G]))
    loads.append(pltpu.make_async_copy(w_hbm.at[:, columns(lax.rem(t + 2, T))], wcol.at[2], load_sem.at[3 + 2 * G]))
    loads.append(pltpu.make_async_copy(hidden_hbm, hid, load_sem.at[2 + 2 * G]))
    for load in loads:
        load.start()

    sub = lax.broadcasted_iota(jnp.int32, (M, M), 0)
    lane = lax.broadcasted_iota(jnp.int32, (M, M), 1)
    eye = sub == lane

    def place_of(owner):
        oz, rest = owner // (NX * NC), lax.rem(owner, NX * NC)
        dz = lax.rem(oz - z + 2 * NZ - NZ // 4, NZ)
        dx = lax.rem(rest // NC - x + NX, NX)
        dc = lax.rem(lax.rem(rest, NC) - c + NC, NC)
        return dz * (NX * NC) + dx * NC + dc

    for load in smalls[:3]:
        load.wait()
    o_row = place_of(owner_ref[...]).astype(F32)
    o_col = column(o_row, eye)
    same = jnp.where(o_row == o_col, 1.0, 0.0)
    rank_row = jnp.sum(jnp.where(sub < lane, same, 0.0), axis=0, keepdims=True)
    rank_col = jnp.sum(jnp.where(lane < sub, same, 0.0), axis=1, keepdims=True)
    owner_id = lax.broadcasted_iota(jnp.int32, (R, M), 0).astype(F32)
    at_owner = owner_id == o_row
    member = slot_ref[...].astype(F32) + 1.0
    queries = q_ref[...]
    for k in range(2):
        pick = jnp.where(at_owner & (rank_row == float(k)), 1.0, 0.0)
        rows = dot(pick.astype(BF16), queries)
        for n in range(4):
            stage[pl.ds(k * 4 + n, R, stride=ROWS), :] = rows[:, n * 128:(n + 1) * 128]
        gid = jnp.sum(pick * member, axis=1, keepdims=True) - 1.0
        stage[pl.ds(8 + k, R, stride=ROWS), :] = jnp.broadcast_to(gid, (R, 128))
    send[...] = stage[...].astype(BF16).reshape(R, ROWS, 128)

    pl.semaphore_wait(barrier, R - 1 + T - 1)

    live = pl.ds(0, LIVE)

    def dispatch(src, dst, send_sem, recv_sem, table, low, high):
        for off in offsets:
            n = index_of(off)
            if low <= n < high:
                pltpu.make_async_remote_copy(
                    src_ref=src.at[n, live], dst_ref=dst.at[n, live], send_sem=send_sem, recv_sem=recv_sem,
                    device_id=(device(table, off), t), device_id_type=MESH,
                ).start()
        if low <= own < high:
            pltpu.make_async_copy(src.at[own, live], dst.at[own, live], recv_sem).start()

    def arrived(dst, recv_sem):
        part = dst.at[pl.ds(0, R), live]
        pltpu.make_async_copy(part, part, recv_sem).wait()

    def departed(src, send_sem):
        part = src.at[pl.ds(0, R - 1), live]
        pltpu.make_async_copy(part, part, send_sem).wait()

    dispatch(send, recv, ssem, rsem, ahead, 0, R)

    part_rows = w_hbm.shape[0] // NC
    my_rows = pl.ds(pl.multiple_of(c * part_rows, part_rows), part_rows)
    sibling = me + 1 - 2 * c
    weights_out = []
    for off in (1, 3):
        to = lax.rem(t + off, T)
        weights_out.append(pltpu.make_async_remote_copy(
            src_ref=w_hbm.at[my_rows, columns(to)], dst_ref=wcol.at[T - off, my_rows], send_sem=wsem.at[off], recv_sem=wrsem.at[T - off],
            device_id=(me, to), device_id_type=MESH,
        ))
        weights_out[-1].start()

    for load in smalls[3:]:
        load.wait()
    qf[...] = queries.astype(F32)
    lenb[...] = jnp.broadcast_to(column(slen_ref[...].astype(F32), eye), lenb.shape)
    loads[0].wait()
    row8 = lax.rem(lax.broadcasted_iota(jnp.int32, (16, 8 * S), 0), 8)
    lanes = lax.broadcasted_iota(jnp.int32, (16, 8 * S), 1)
    own_row = lanes // S == row8
    place = lax.rem(lanes, S).astype(F32)
    for b in range(M // 8):
        q8 = qf[8 * b:8 * b + 8, :]
        both = jnp.concatenate([q8[:, :HD], q8[:, HD:]], axis=0).astype(BF16)
        length = lenb[8 * b:8 * b + 8, :]
        length = jnp.concatenate([length, length], axis=0)
        keys = sfx[8 * b:8 * b + 8, 0].reshape(8 * S, HD)
        values = sfx[8 * b:8 * b + 8, 1].reshape(8 * S, HD)
        weights = jnp.where(own_row & (place < length), capped_exp(nt(both, keys)), 0.0)
        den = jnp.sum(weights, axis=1, keepdims=True)
        num = dot(weights.astype(BF16), values)
        for h in range(2):
            num_s[8 * b:8 * b + 8, h * HD:(h + 1) * HD] = num[8 * h:8 * h + 8, :]
            den_s[8 * b:8 * b + 8, h * HD:(h + 1) * HD] = jnp.broadcast_to(den[8 * h:8 * h + 8, :], (8, HD))
    for load in loads[1:1 + 2 * G]:
        load.wait()

    arrived(recv, rsem)
    stage[...] = recv[...].reshape(R * ROWS, 128).astype(F32)
    CH = 512
    rows, gid = [], []
    for part in range(PARTS):
        def chunk(n):
            return stage[pl.ds(part * H * ROWS + n, H, stride=ROWS), :]

        for k in range(2):
            for h in range(2):
                rows.append(jnp.concatenate([chunk(k * 4 + 2 * h), chunk(k * 4 + 2 * h + 1)], axis=1))
                gid.append(chunk(8 + k))
    rows, gid = jnp.concatenate(rows, axis=0), jnp.concatenate(gid, axis=0)
    gid2 = jnp.concatenate([gid, gid], axis=1)
    length = jnp.zeros(gid.shape, jnp.int32)
    for g in range(G):
        qsel[g] = jnp.where(gid2 == float(g), rows, 0.0).astype(BF16)
        length = jnp.where(gid == float(g), plen_ref[0:1, g:g + 1], length)
    length4 = jnp.concatenate([length] * (CH // 128), axis=1)
    total_den = jnp.zeros((4 * R, 1), F32)
    for p in range(size // CH):
        scores = nt(qsel[0], kv[0, 0, p * CH:(p + 1) * CH, :])
        for g in range(1, G):
            scores = scores + nt(qsel[g], kv[g, 0, p * CH:(p + 1) * CH, :])
        position = lax.broadcasted_iota(jnp.int32, scores.shape, 1) + p * CH
        weights = jnp.where(position < length4, capped_exp(scores), 0.0)
        total_den = total_den + jnp.sum(weights, axis=1, keepdims=True)
        wts[:, p * CH:(p + 1) * CH] = weights.astype(BF16)
    high = total_den.astype(BF16).astype(F32)
    low = total_den - high
    safe = jnp.where(total_den > 0.0, total_den, 1.0)
    quarter = lax.broadcasted_iota(jnp.int32, (H, 128), 1) // 32
    for part in range(PARTS):
        first = part * H
        these = slice(4 * first, 4 * (first + H))
        num = jnp.zeros((4 * H, HD), F32)
        for g in range(G):
            num = jnp.where(gid2[these] == float(g), dot(wts[these, :], kv[g, 1]), num)
        mean = num / safe[these]
        for k in range(2):
            dens = jnp.zeros((H, 128), F32)
            for h in range(2):
                at = slice((k * 2 + h) * H, (k * 2 + h + 1) * H)
                stage_out[pl.ds(first * ROWS + k * 4 + 2 * h, H, stride=ROWS), :] = mean[at, :128]
                stage_out[pl.ds(first * ROWS + k * 4 + 2 * h + 1, H, stride=ROWS), :] = mean[at, 128:]
                dens = jnp.where(quarter == 2 * h, high[these][at], jnp.where(quarter == 2 * h + 1, low[these][at], dens))
            stage_out[pl.ds(first * ROWS + 8 + k, H, stride=ROWS), :] = dens
        back[first:first + H] = stage_out[first * ROWS:(first + H) * ROWS, :].astype(BF16).reshape(H, ROWS, 128)
        dispatch(back, ret, bsem, tsem, behind, first, first + H)

    spot = lax.broadcasted_iota(jnp.int32, (M, 2 * R), 1).astype(F32)
    fetch = jnp.where(spot == rank_col * float(R) + o_col, 1.0, 0.0).astype(BF16)
    loads[1 + 2 * G].wait()
    loads[2 + 2 * G].wait()
    loads[3 + 2 * G].wait()
    arrived(ret, tsem)
    stage[...] = ret[...].reshape(R * ROWS, 128).astype(F32)

    def answers(n):
        return stage[pl.ds(n, R, stride=ROWS), :]

    table = jnp.concatenate(
        [jnp.concatenate([answers(n) for n in (k * 4, k * 4 + 1, k * 4 + 2, k * 4 + 3, 8 + k)], axis=1) for k in range(2)], axis=0
    ).astype(BF16)
    mine = dot(fetch, table)
    parts = []
    for h in range(2):
        den_p = mine[:, 512 + 64 * h:513 + 64 * h] + mine[:, 544 + 64 * h:545 + 64 * h]
        cols = slice(h * HD, (h + 1) * HD)
        parts.append((mine[:, cols] * den_p + num_s[:, cols]) / (den_p + den_s[:, cols]))
    attention = jnp.concatenate(parts, axis=1).astype(BF16)

    atts[0] = attention
    given = []
    for off in (1, 3):
        given.append(pltpu.make_async_remote_copy(
            src_ref=atts.at[0], dst_ref=atts.at[T - off], send_sem=psem.at[off], recv_sem=prsem.at[T - off],
            device_id=(me, lax.rem(t + off, T)), device_id_type=MESH,
        ))
        given[-1].start()
    far[0] = dot(attention, wcol[2]).astype(BF16)
    given.append(pltpu.make_async_remote_copy(
        src_ref=far.at[0], dst_ref=far.at[1], send_sem=psem.at[2], recv_sem=prsem.at[2],
        device_id=(me, lax.rem(t + 2, T)), device_id_type=MESH,
    ))
    given[-1].start()
    passed = []
    for off in (1, 3):
        pltpu.make_async_copy(wcol.at[off, my_rows], wcol.at[off, my_rows], wrsem.at[off]).wait()
        passed.append(pltpu.make_async_remote_copy(
            src_ref=wcol.at[off, my_rows], dst_ref=wcol.at[off, my_rows], send_sem=fsem.at[off], recv_sem=frsem.at[off],
            device_id=(sibling, t), device_id_type=MESH,
        ))
        passed[-1].start()
    total = dot(attention, wcol[0])
    for n, off in enumerate((1, 3)):
        passed[n].wait_recv()
        pltpu.make_async_copy(atts.at[off], atts.at[off], prsem.at[off]).wait()
        total = total + dot(atts[off], wcol[off])
    given[-1].wait_recv()
    total = total + far[1].astype(F32)

    square = jnp.sum(total * total, axis=1, keepdims=True)
    eye_wide = lax.broadcasted_iota(jnp.int32, (M, 128), 0) == lax.broadcasted_iota(jnp.int32, (M, 128), 1)
    square_row = jnp.sum(jnp.where(eye_wide, square, 0.0), axis=0, keepdims=True)
    sqsend[...] = jnp.broadcast_to(square_row, (8, 128))
    squares = []
    for off in (2, 1, 3):
        squares.append(pltpu.make_async_remote_copy(
            src_ref=sqsend, dst_ref=sqrecv.at[off], send_sem=qsem.at[off], recv_sem=qrsem.at[off],
            device_id=(me, lax.rem(t + off, T)), device_id_type=MESH,
        ))
        squares[-1].start()
    scaled = total * gain_ref[...].reshape(1, width)
    departed(send, ssem)
    departed(back, bsem)
    for copy in squares:
        copy.wait_recv()
    for off in range(1, T):
        square_row = square_row + sqrecv[off, 0:1, :]
    mean_square = column(square_row, eye_wide) * (1.0 / (width * T))
    out_ref[...] = (hid[...].astype(F32) + scaled * lax.rsqrt(mean_square + EPSILON)).astype(BF16)

    for copy in weights_out + given + passed + squares:
        copy.wait_send()


def shards(
    hidden_input, queries, prompt_cache, suffix_cache, owner_replica, group_slot, prompt_length, suffix_length,
    output_weight, post_gain,
):
    R, T = lax.axis_size("replica"), lax.axis_size("tensor")
    M, width = hidden_input.shape
    G, _, size, _ = prompt_cache.shape
    S = suffix_cache.shape[2]
    vmem = pl.BlockSpec(memory_space=pltpu.VMEM)
    hbm = pl.BlockSpec(memory_space=pl.ANY)
    dma = pltpu.SemaphoreType.DMA
    message = pltpu.VMEM((R, ROWS, 128), BF16)
    return pl.pallas_call(
        functools.partial(kernel, R, T, M, width),
        out_shape=jax.ShapeDtypeStruct((M, width), BF16),
        in_specs=[hbm] * 10,
        out_specs=vmem,
        scratch_shapes=[
            pltpu.VMEM((1, M), jnp.int32), pltpu.VMEM((1, M), jnp.int32), pltpu.VMEM((1, M), jnp.int32), pltpu.VMEM((1, G), jnp.int32),
            pltpu.VMEM((width,), F32), pltpu.VMEM(queries.shape, BF16),
            pltpu.VMEM(prompt_cache.shape, BF16),
            pltpu.VMEM(suffix_cache.shape, BF16),
            pltpu.VMEM((T, output_weight.shape[0], width), BF16),
            pltpu.VMEM((M, width), BF16),
            message, message, message, message,
            pltpu.VMEM((R * ROWS, 128), F32),
            pltpu.VMEM((R * ROWS, 128), F32),
            pltpu.VMEM((M, 2 * HD), F32),
            pltpu.VMEM((M, 8 * S), F32),
            pltpu.VMEM((G, 4 * R, HD), BF16),
            pltpu.VMEM((4 * R, size), BF16),
            pltpu.VMEM((M, 2 * HD), F32),
            pltpu.VMEM((M, 2 * HD), F32),
            pltpu.VMEM((T, M, 2 * HD), BF16),
            pltpu.VMEM((2, M, width), BF16),
            pltpu.VMEM((8, 128), F32),
            pltpu.VMEM((T, 8, 128), F32),
            dma((6,)), dma((4 + 2 * G,)), dma(()), dma(()), dma(()), dma(()), *[dma((T,))] * 8,
        ],
        compiler_params=pltpu.CompilerParams(collective_id=0, has_side_effects=True, vmem_limit_bytes=56 * 2 ** 20),
        name="decode_attention",
    )(
        owner_replica.reshape(1, M), group_slot.reshape(1, M), suffix_length.reshape(1, M), prompt_length.reshape(1, G),
        post_gain, queries, hidden_input, prompt_cache, suffix_cache, output_weight,
    )


def solution(mesh):
    in_specs = (
        P("replica", "tensor"), P("replica", "tensor"), P("replica", None, None, "tensor"), P("replica", None, None, "tensor"),
        P("replica", None), P("replica"), P("replica"), P("replica"), P("tensor", None), P("tensor"),
    )
    return jax.shard_map(shards, mesh=mesh, in_specs=in_specs, out_specs=P("replica", "tensor"), check_vma=False)
```

```python
import functools

import jax
import jax.numpy as jnp
from jax import lax
from jax.experimental import pallas as pl
from jax.experimental.pallas import tpu as pltpu
from jax.sharding import PartitionSpec as P

MESH = pl.DeviceIdType.MESH
HD = 256
PARTS = 2
ROWS = 16
LIVE = 10
SOFTCAP = 50.0
EPSILON = 1e-06
F32, BF16 = jnp.float32, jnp.bfloat16


def capped_exp(scores):
    return jnp.exp(SOFTCAP * jnp.tanh(scores * (HD ** -0.5 / SOFTCAP)))


def nt(a, b):
    return lax.dot_general(a, b, (((1,), (1,)), ((), ())), preferred_element_type=F32)


def dot(a, b):
    return jnp.dot(a, b, preferred_element_type=F32)


def column(row, eye):
    return jnp.sum(jnp.where(eye, row, 0.0), axis=1, keepdims=True)


def grid_of(R):
    return (R // 8, 4, 2) if R >= 64 else (R // 2, 1, 2)


def hops(off, dims):
    return sum(min(o, n - o) * w for o, n, w in zip(off, dims, (1.0, 1.0, 0.5)))


def kernel(
    R, T, M, width,
    owner_hbm, slot_hbm, slen_hbm, plen_hbm, gain_hbm, q_hbm, hidden_hbm, prompt_hbm, suffix_hbm, w_hbm,
    out_ref,
    owner_ref, slot_ref, slen_ref, plen_ref, gain_ref, q_ref,
    kv, sfx, wcol, hid, send, recv, back, ret, stage, stage_out, qf, lenb, qsel, wts, num_s, den_s,
    atts, far, sqsend, sqrecv,
    small_sem, load_sem, ssem, rsem, bsem, tsem, psem, prsem, wsem, wrsem, fsem, frsem, qsem, qrsem,
):
    me, t = lax.axis_index("replica"), lax.axis_index("tensor")
    G, _, size, _ = kv.shape
    S = sfx.shape[2]
    NZ, NX, NC = dims = grid_of(R)
    H = R // PARTS

    smalls = [
        pltpu.make_async_copy(src, dst, small_sem.at[n])
        for n, (src, dst) in enumerate((
            (owner_hbm, owner_ref), (slot_hbm, slot_ref), (q_hbm, q_ref), (slen_hbm, slen_ref), (plen_hbm, plen_ref), (gain_hbm, gain_ref),
        ))
    ]
    for load in smalls:
        load.start()

    z, x, c = me // (NX * NC), lax.rem(me // NC, NX), lax.rem(me, NC)
    ahead = [[lax.rem(p + o, n) for o in range(n)] for p, n in ((z, NZ), (x, NX), (c, NC))]
    behind = [[lax.rem(p + n - o, n) for o in range(n)] for p, n in ((z, NZ), (x, NX), (c, NC))]
    offsets = [(lax_z, lax_x, lax_c) for lax_z in range(NZ) for lax_x in range(NX) for lax_c in range(NC)]
    offsets = sorted(offsets, key=lambda off: -hops(off, dims))[:-1]

    def index_of(off):
        return ((off[0] + NZ - NZ // 4) % NZ) * NX * NC + off[1] * NC + off[2]

    def device(table, off):
        return table[0][off[0]] * (NX * NC) + table[1][off[1]] * NC + table[2][off[2]]

    own = index_of((0, 0, 0))

    barrier = pltpu.get_barrier_semaphore()
    for off in offsets:
        pl.semaphore_signal(barrier, inc=1, device_id=(device(ahead, off), t), device_id_type=MESH)
    for off in range(1, T):
        pl.semaphore_signal(barrier, inc=1, device_id=(me, lax.rem(t + off, T)), device_id_type=MESH)

    loads = [pltpu.make_async_copy(suffix_hbm, sfx, load_sem.at[0])]
    for a in range(2):
        for g in range(G):
            loads.append(pltpu.make_async_copy(prompt_hbm.at[g, a], kv.at[g, a], load_sem.at[1 + a * G + g]))
    def columns(which):
        return pl.ds(pl.multiple_of(which * width, 128), width)

    loads.append(pltpu.make_async_copy(w_hbm.at[:, columns(t)], wcol.at[0], load_sem.at[1 + 2 * G]))
    loads.append(pltpu.make_async_copy(w_hbm.at[:, columns(lax.rem(t + 2, T))], wcol.at[2], load_sem.at[3 + 2 * G]))
    loads.append(pltpu.make_async_copy(hidden_hbm, hid, load_sem.at[2 + 2 * G]))
    for load in loads:
        load.start()

    sub = lax.broadcasted_iota(jnp.int32, (M, M), 0)
    lane = lax.broadcasted_iota(jnp.int32, (M, M), 1)
    eye = sub == lane

    def place_of(owner):
        oz, rest = owner // (NX * NC), lax.rem(owner, NX * NC)
        dz = lax.rem(oz - z + 2 * NZ - NZ // 4, NZ)
        dx = lax.rem(rest // NC - x + NX, NX)
        dc = lax.rem(lax.rem(rest, NC) - c + NC, NC)
        return dz * (NX * NC) + dx * NC + dc

    for load in smalls[:3]:
        load.wait()
    o_row = place_of(owner_ref[...]).astype(F32)
    o_col = column(o_row, eye)
    same = jnp.where(o_row == o_col, 1.0, 0.0)
    rank_row = jnp.sum(jnp.where(sub < lane, same, 0.0), axis=0, keepdims=True)
    rank_col = jnp.sum(jnp.where(lane < sub, same, 0.0), axis=1, keepdims=True)
    owner_id = lax.broadcasted_iota(jnp.int32, (R, M), 0).astype(F32)
    at_owner = owner_id == o_row
    member = slot_ref[...].astype(F32) + 1.0
    queries = q_ref[...]
    for k in range(2):
        pick = jnp.where(at_owner & (rank_row == float(k)), 1.0, 0.0)
        rows = dot(pick.astype(BF16), queries)
        for n in range(4):
            stage[pl.ds(k * 4 + n, R, stride=ROWS), :] = rows[:, n * 128:(n + 1) * 128]
        gid = jnp.sum(pick * member, axis=1, keepdims=True) - 1.0
        stage[pl.ds(8 + k, R, stride=ROWS), :] = jnp.broadcast_to(gid, (R, 128))
    send[...] = stage[...].astype(BF16).reshape(R, ROWS, 128)

    pl.semaphore_wait(barrier, R - 1 + T - 1)

    live = pl.ds(0, LIVE)

    def dispatch(src, dst, send_sem, recv_sem, table, low, high):
        for off in offsets:
            n = index_of(off)
            if low <= n < high:
                pltpu.make_async_remote_copy(
                    src_ref=src.at[n, live], dst_ref=dst.at[n, live], send_sem=send_sem, recv_sem=recv_sem,
                    device_id=(device(table, off), t), device_id_type=MESH,
                ).start()
        if low <= own < high:
            pltpu.make_async_copy(src.at[own, live], dst.at[own, live], recv_sem).start()

    def arrived(dst, recv_sem):
        part = dst.at[pl.ds(0, R), live]
        pltpu.make_async_copy(part, part, recv_sem).wait()

    def departed(src, send_sem):
        part = src.at[pl.ds(0, R - 1), live]
        pltpu.make_async_copy(part, part, send_sem).wait()

    dispatch(send, recv, ssem, rsem, ahead, 0, R)

    part_rows = w_hbm.shape[0] // NC
    my_rows = pl.ds(pl.multiple_of(c * part_rows, part_rows), part_rows)
    sibling = me + 1 - 2 * c
    weights_out = []
    for off in (1, 3):
        to = lax.rem(t + off, T)
        weights_out.append(pltpu.make_async_remote_copy(
            src_ref=w_hbm.at[my_rows, columns(to)], dst_ref=wcol.at[T - off, my_rows], send_sem=wsem.at[off], recv_sem=wrsem.at[T - off],
            device_id=(me, to), device_id_type=MESH,
        ))
        weights_out[-1].start()

    for load in smalls[3:]:
        load.wait()
    qf[...] = queries.astype(F32)
    lenb[...] = jnp.broadcast_to(column(slen_ref[...].astype(F32), eye), lenb.shape)
    loads[0].wait()
    row8 = lax.rem(lax.broadcasted_iota(jnp.int32, (16, 8 * S), 0), 8)
    lanes = lax.broadcasted_iota(jnp.int32, (16, 8 * S), 1)
    own_row = lanes // S == row8
    place = lax.rem(lanes, S).astype(F32)
    for b in range(M // 8):
        q8 = qf[8 * b:8 * b + 8, :]
        both = jnp.concatenate([q8[:, :HD], q8[:, HD:]], axis=0).astype(BF16)
        length = lenb[8 * b:8 * b + 8, :]
        length = jnp.concatenate([length, length], axis=0)
        keys = sfx[8 * b:8 * b + 8, 0].reshape(8 * S, HD)
        values = sfx[8 * b:8 * b + 8, 1].reshape(8 * S, HD)
        weights = jnp.where(own_row & (place < length), capped_exp(nt(both, keys)), 0.0)
        den = jnp.sum(weights, axis=1, keepdims=True)
        num = dot(weights.astype(BF16), values)
        for h in range(2):
            num_s[8 * b:8 * b + 8, h * HD:(h + 1) * HD] = num[8 * h:8 * h + 8, :]
            den_s[8 * b:8 * b + 8, h * HD:(h + 1) * HD] = jnp.broadcast_to(den[8 * h:8 * h + 8, :], (8, HD))
    for load in loads[1:1 + 2 * G]:
        load.wait()

    arrived(recv, rsem)
    stage[...] = recv[...].reshape(R * ROWS, 128).astype(F32)
    CH = 512
    rows, gid = [], []
    for part in range(PARTS):
        def chunk(n):
            return stage[pl.ds(part * H * ROWS + n, H, stride=ROWS), :]

        for k in range(2):
            for h in range(2):
                rows.append(jnp.concatenate([chunk(k * 4 + 2 * h), chunk(k * 4 + 2 * h + 1)], axis=1))
                gid.append(chunk(8 + k))
    rows, gid = jnp.concatenate(rows, axis=0), jnp.concatenate(gid, axis=0)
    gid2 = jnp.concatenate([gid, gid], axis=1)
    length = jnp.zeros(gid.shape, jnp.int32)
    for g in range(G):
        qsel[g] = jnp.where(gid2 == float(g), rows, 0.0).astype(BF16)
        length = jnp.where(gid == float(g), plen_ref[0:1, g:g + 1], length)
    length4 = jnp.concatenate([length] * (CH // 128), axis=1)
    total_den = jnp.zeros((4 * R, 1), F32)
    for p in range(size // CH):
        scores = nt(qsel[0], kv[0, 0, p * CH:(p + 1) * CH, :])
        for g in range(1, G):
            scores = scores + nt(qsel[g], kv[g, 0, p * CH:(p + 1) * CH, :])
        position = lax.broadcasted_iota(jnp.int32, scores.shape, 1) + p * CH
        weights = jnp.where(position < length4, capped_exp(scores), 0.0)
        total_den = total_den + jnp.sum(weights, axis=1, keepdims=True)
        wts[:, p * CH:(p + 1) * CH] = weights.astype(BF16)
    high = total_den.astype(BF16).astype(F32)
    low = total_den - high
    safe = jnp.where(total_den > 0.0, total_den, 1.0)
    quarter = lax.broadcasted_iota(jnp.int32, (H, 128), 1) // 32
    for part in range(PARTS):
        first = part * H
        these = slice(4 * first, 4 * (first + H))
        num = jnp.zeros((4 * H, HD), F32)
        for g in range(G):
            num = jnp.where(gid2[these] == float(g), dot(wts[these, :], kv[g, 1]), num)
        mean = num / safe[these]
        for k in range(2):
            dens = jnp.zeros((H, 128), F32)
            for h in range(2):
                at = slice((k * 2 + h) * H, (k * 2 + h + 1) * H)
                stage_out[pl.ds(first * ROWS + k * 4 + 2 * h, H, stride=ROWS), :] = mean[at, :128]
                stage_out[pl.ds(first * ROWS + k * 4 + 2 * h + 1, H, stride=ROWS), :] = mean[at, 128:]
                dens = jnp.where(quarter == 2 * h, high[these][at], jnp.where(quarter == 2 * h + 1, low[these][at], dens))
            stage_out[pl.ds(first * ROWS + 8 + k, H, stride=ROWS), :] = dens
        back[first:first + H] = stage_out[first * ROWS:(first + H) * ROWS, :].astype(BF16).reshape(H, ROWS, 128)
        dispatch(back, ret, bsem, tsem, behind, first, first + H)

    spot = lax.broadcasted_iota(jnp.int32, (M, 2 * R), 1).astype(F32)
    fetch = jnp.where(spot == rank_col * float(R) + o_col, 1.0, 0.0).astype(BF16)
    loads[1 + 2 * G].wait()
    loads[2 + 2 * G].wait()
    loads[3 + 2 * G].wait()
    arrived(ret, tsem)
    stage[...] = ret[...].reshape(R * ROWS, 128).astype(F32)

    def answers(n):
        return stage[pl.ds(n, R, stride=ROWS), :]

    table = jnp.concatenate(
        [jnp.concatenate([answers(n) for n in (k * 4, k * 4 + 1, k * 4 + 2, k * 4 + 3, 8 + k)], axis=1) for k in range(2)], axis=0
    ).astype(BF16)
    mine = dot(fetch, table)
    parts = []
    for h in range(2):
        den_p = mine[:, 512 + 64 * h:513 + 64 * h] + mine[:, 544 + 64 * h:545 + 64 * h]
        cols = slice(h * HD, (h + 1) * HD)
        parts.append((mine[:, cols] * den_p + num_s[:, cols]) / (den_p + den_s[:, cols]))
    attention = jnp.concatenate(parts, axis=1).astype(BF16)

    atts[0] = attention
    given = []
    for off in (1, 3):
        given.append(pltpu.make_async_remote_copy(
            src_ref=atts.at[0], dst_ref=atts.at[T - off], send_sem=psem.at[off], recv_sem=prsem.at[T - off],
            device_id=(me, lax.rem(t + off, T)), device_id_type=MESH,
        ))
        given[-1].start()
    far[0] = dot(attention, wcol[2]).astype(BF16)
    given.append(pltpu.make_async_remote_copy(
        src_ref=far.at[0], dst_ref=far.at[1], send_sem=psem.at[2], recv_sem=prsem.at[2],
        device_id=(me, lax.rem(t + 2, T)), device_id_type=MESH,
    ))
    given[-1].start()
    passed = []
    for off in (1, 3):
        pltpu.make_async_copy(wcol.at[off, my_rows], wcol.at[off, my_rows], wrsem.at[off]).wait()
        passed.append(pltpu.make_async_remote_copy(
            src_ref=wcol.at[off, my_rows], dst_ref=wcol.at[off, my_rows], send_sem=fsem.at[off], recv_sem=frsem.at[off],
            device_id=(sibling, t), device_id_type=MESH,
        ))
        passed[-1].start()
    total = dot(attention, wcol[0])
    for n, off in enumerate((1, 3)):
        passed[n].wait_recv()
        pltpu.make_async_copy(atts.at[off], atts.at[off], prsem.at[off]).wait()
        total = total + dot(atts[off], wcol[off])
    given[-1].wait_recv()
    total = total + far[1].astype(F32)

    square = jnp.sum(total * total, axis=1, keepdims=True)
    eye_wide = lax.broadcasted_iota(jnp.int32, (M, 128), 0) == lax.broadcasted_iota(jnp.int32, (M, 128), 1)
    square_row = jnp.sum(jnp.where(eye_wide, square, 0.0), axis=0, keepdims=True)
    sqsend[...] = jnp.broadcast_to(square_row, (8, 128))
    squares = []
    for off in (2, 1, 3):
        squares.append(pltpu.make_async_remote_copy(
            src_ref=sqsend, dst_ref=sqrecv.at[off], send_sem=qsem.at[off], recv_sem=qrsem.at[off],
            device_id=(me, lax.rem(t + off, T)), device_id_type=MESH,
        ))
        squares[-1].start()
    scaled = total * gain_ref[...].reshape(1, width)
    departed(send, ssem)
    departed(back, bsem)
    for copy in squares:
        copy.wait_recv()
    for off in range(1, T):
        square_row = square_row + sqrecv[off, 0:1, :]
    mean_square = column(square_row, eye_wide) * (1.0 / (width * T))
    out_ref[...] = (hid[...].astype(F32) + scaled * lax.rsqrt(mean_square + EPSILON)).astype(BF16)

    for copy in weights_out + given + passed + squares:
        copy.wait_send()


def shards(
    hidden_input, queries, prompt_cache, suffix_cache, owner_replica, group_slot, prompt_length, suffix_length,
    output_weight, post_gain,
):
    R, T = lax.axis_size("replica"), lax.axis_size("tensor")
    M, width = hidden_input.shape
    G, _, size, _ = prompt_cache.shape
    S = suffix_cache.shape[2]
    vmem = pl.BlockSpec(memory_space=pltpu.VMEM)
    hbm = pl.BlockSpec(memory_space=pl.ANY)
    dma = pltpu.SemaphoreType.DMA
    message = pltpu.VMEM((R, ROWS, 128), BF16)
    result = pl.pallas_call(
        functools.partial(kernel, R, T, M, width),
        out_shape=pltpu.VMEM((M, width), BF16),
        in_specs=[hbm] * 10,
        out_specs=vmem,
        scratch_shapes=[
            pltpu.VMEM((1, M), jnp.int32), pltpu.VMEM((1, M), jnp.int32), pltpu.VMEM((1, M), jnp.int32), pltpu.VMEM((1, G), jnp.int32),
            pltpu.VMEM((width,), F32), pltpu.VMEM(queries.shape, BF16),
            pltpu.VMEM(prompt_cache.shape, BF16),
            pltpu.VMEM(suffix_cache.shape, BF16),
            pltpu.VMEM((T, output_weight.shape[0], width), BF16),
            pltpu.VMEM((M, width), BF16),
            message, message, message, message,
            pltpu.VMEM((R * ROWS, 128), F32),
            pltpu.VMEM((R * ROWS, 128), F32),
            pltpu.VMEM((M, 2 * HD), F32),
            pltpu.VMEM((M, 8 * S), F32),
            pltpu.VMEM((G, 4 * R, HD), BF16),
            pltpu.VMEM((4 * R, size), BF16),
            pltpu.VMEM((M, 2 * HD), F32),
            pltpu.VMEM((M, 2 * HD), F32),
            pltpu.VMEM((T, M, 2 * HD), BF16),
            pltpu.VMEM((2, M, width), BF16),
            pltpu.VMEM((8, 128), F32),
            pltpu.VMEM((T, 8, 128), F32),
            dma((6,)), dma((4 + 2 * G,)), dma(()), dma(()), dma(()), dma(()), *[dma((T,))] * 8,
        ],
        compiler_params=pltpu.CompilerParams(collective_id=0, has_side_effects=True, vmem_limit_bytes=56 * 2 ** 20),
        name="decode_attention",
    )(
        owner_replica.reshape(1, M), group_slot.reshape(1, M), suffix_length.reshape(1, M), prompt_length.reshape(1, G),
        post_gain, queries, hidden_input, prompt_cache, suffix_cache, output_weight,
    )

    return result


def solution(mesh):
    in_specs = (
        P("replica", "tensor"), P("replica", "tensor"), P("replica", None, None, "tensor"), P("replica", None, None, "tensor"),
        P("replica", None), P("replica"), P("replica"), P("replica"), P("tensor", None), P("tensor"),
    )
    return jax.shard_map(shards, mesh=mesh, in_specs=in_specs, out_specs=P("replica", "tensor"), check_vma=False)
```

```python
import functools

import jax
import jax.numpy as jnp
from jax import lax
from jax.experimental import pallas as pl
from jax.experimental.pallas import tpu as pltpu
from jax.sharding import PartitionSpec as P

MESH = pl.DeviceIdType.MESH
HD = 256
PARTS = 2
ROWS = 16
LIVE = 10
SOFTCAP = 50.0
EPSILON = 1e-06
F32, BF16 = jnp.float32, jnp.bfloat16


def capped_exp(scores):
    return jnp.exp(SOFTCAP * jnp.tanh(scores * (HD ** -0.5 / SOFTCAP)))


def nt(a, b):
    return lax.dot_general(a, b, (((1,), (1,)), ((), ())), preferred_element_type=F32)


def dot(a, b):
    return jnp.dot(a, b, preferred_element_type=F32)


def column(row, eye):
    return jnp.sum(jnp.where(eye, row, 0.0), axis=1, keepdims=True)


def grid_of(R):
    return (R // 8, 4, 2) if R >= 64 else (R // 2, 1, 2)


def hops(off, dims):
    return sum(min(o, n - o) * w for o, n, w in zip(off, dims, (1.0, 1.6, 0.5)))


def kernel(
    R, T, M, width,
    owner_hbm, slot_hbm, slen_hbm, plen_hbm, gain_hbm, q_hbm, hidden_hbm, prompt_hbm, suffix_hbm, w_hbm,
    out_ref,
    owner_ref, slot_ref, slen_ref, plen_ref, gain_ref, q_ref,
    kv, sfx, wcol, hid, send, recv, back, ret, stage, stage_out, qf, lenb, qsel, wts, num_s, den_s,
    atts, far, sqsend, sqrecv,
    small_sem, load_sem, ssem, rsem, bsem, tsem, psem, prsem, wsem, wrsem, fsem, frsem, qsem, qrsem,
):
    me, t = lax.axis_index("replica"), lax.axis_index("tensor")
    G, _, size, _ = kv.shape
    S = sfx.shape[2]
    NZ, NX, NC = dims = grid_of(R)
    H = R // PARTS

    smalls = [
        pltpu.make_async_copy(src, dst, small_sem.at[n])
        for n, (src, dst) in enumerate((
            (owner_hbm, owner_ref), (slot_hbm, slot_ref), (q_hbm, q_ref), (slen_hbm, slen_ref), (plen_hbm, plen_ref), (gain_hbm, gain_ref),
        ))
    ]
    for load in smalls:
        load.start()

    z, x, c = me // (NX * NC), lax.rem(me // NC, NX), lax.rem(me, NC)
    ahead = [[lax.rem(p + o, n) for o in range(n)] for p, n in ((z, NZ), (x, NX), (c, NC))]
    behind = [[lax.rem(p + n - o, n) for o in range(n)] for p, n in ((z, NZ), (x, NX), (c, NC))]
    offsets = [(lax_z, lax_x, lax_c) for lax_z in range(NZ) for lax_x in range(NX) for lax_c in range(NC)]
    offsets = sorted(offsets, key=lambda off: -hops(off, dims))[:-1]

    def index_of(off):
        return ((off[0] + NZ - NZ // 4) % NZ) * NX * NC + off[1] * NC + off[2]

    def device(table, off):
        return table[0][off[0]] * (NX * NC) + table[1][off[1]] * NC + table[2][off[2]]

    own = index_of((0, 0, 0))

    barrier = pltpu.get_barrier_semaphore()
    for off in offsets:
        pl.semaphore_signal(barrier, inc=1, device_id=(device(ahead, off), t), device_id_type=MESH)
    for off in range(1, T):
        pl.semaphore_signal(barrier, inc=1, device_id=(me, lax.rem(t + off, T)), device_id_type=MESH)

    loads = [pltpu.make_async_copy(suffix_hbm, sfx, load_sem.at[0])]
    for a in range(2):
        for g in range(G):
            loads.append(pltpu.make_async_copy(prompt_hbm.at[g, a], kv.at[g, a], load_sem.at[1 + a * G + g]))
    def columns(which):
        return pl.ds(pl.multiple_of(which * width, 128), width)

    loads.append(pltpu.make_async_copy(w_hbm.at[:, columns(t)], wcol.at[0], load_sem.at[1 + 2 * G]))
    loads.append(pltpu.make_async_copy(w_hbm.at[:, columns(lax.rem(t + 2, T))], wcol.at[2], load_sem.at[3 + 2 * G]))
    loads.append(pltpu.make_async_copy(hidden_hbm, hid, load_sem.at[2 + 2 * G]))
    for load in loads:
        load.start()

    sub = lax.broadcasted_iota(jnp.int32, (M, M), 0)
    lane = lax.broadcasted_iota(jnp.int32, (M, M), 1)
    eye = sub == lane

    def place_of(owner):
        oz, rest = owner // (NX * NC), lax.rem(owner, NX * NC)
        dz = lax.rem(oz - z + 2 * NZ - NZ // 4, NZ)
        dx = lax.rem(rest // NC - x + NX, NX)
        dc = lax.rem(lax.rem(rest, NC) - c + NC, NC)
        return dz * (NX * NC) + dx * NC + dc

    for load in smalls[:3]:
        load.wait()
    o_row = place_of(owner_ref[...]).astype(F32)
    o_col = column(o_row, eye)
    same = jnp.where(o_row == o_col, 1.0, 0.0)
    rank_row = jnp.sum(jnp.where(sub < lane, same, 0.0), axis=0, keepdims=True)
    rank_col = jnp.sum(jnp.where(lane < sub, same, 0.0), axis=1, keepdims=True)
    owner_id = lax.broadcasted_iota(jnp.int32, (R, M), 0).astype(F32)
    at_owner = owner_id == o_row
    member = slot_ref[...].astype(F32) + 1.0
    queries = q_ref[...]
    for k in range(2):
        pick = jnp.where(at_owner & (rank_row == float(k)), 1.0, 0.0)
        rows = dot(pick.astype(BF16), queries)
        for n in range(4):
            stage[pl.ds(k * 4 + n, R, stride=ROWS), :] = rows[:, n * 128:(n + 1) * 128]
        gid = jnp.sum(pick * member, axis=1, keepdims=True) - 1.0
        stage[pl.ds(8 + k, R, stride=ROWS), :] = jnp.broadcast_to(gid, (R, 128))
    send[...] = stage[...].astype(BF16).reshape(R, ROWS, 128)

    pl.semaphore_wait(barrier, R - 1 + T - 1)

    live = pl.ds(0, LIVE)

    def dispatch(src, dst, send_sem, recv_sem, table, low, high):
        for off in offsets:
            n = index_of(off)
            if low <= n < high:
                pltpu.make_async_remote_copy(
                    src_ref=src.at[n, live], dst_ref=dst.at[n, live], send_sem=send_sem, recv_sem=recv_sem,
                    device_id=(device(table, off), t), device_id_type=MESH,
                ).start()
        if low <= own < high:
            pltpu.make_async_copy(src.at[own, live], dst.at[own, live], recv_sem).start()

    def arrived(dst, recv_sem):
        part = dst.at[pl.ds(0, R), live]
        pltpu.make_async_copy(part, part, recv_sem).wait()

    def departed(src, send_sem):
        part = src.at[pl.ds(0, R - 1), live]
        pltpu.make_async_copy(part, part, send_sem).wait()

    dispatch(send, recv, ssem, rsem, ahead, 0, R)

    part_rows = w_hbm.shape[0] // NC
    my_rows = pl.ds(pl.multiple_of(c * part_rows, part_rows), part_rows)
    sibling = me + 1 - 2 * c
    weights_out = []
    for off in (1, 3):
        to = lax.rem(t + off, T)
        weights_out.append(pltpu.make_async_remote_copy(
            src_ref=w_hbm.at[my_rows, columns(to)], dst_ref=wcol.at[T - off, my_rows], send_sem=wsem.at[off], recv_sem=wrsem.at[T - off],
            device_id=(me, to), device_id_type=MESH,
        ))
        weights_out[-1].start()

    for load in smalls[3:]:
        load.wait()
    qf[...] = queries.astype(F32)
    lenb[...] = jnp.broadcast_to(column(slen_ref[...].astype(F32), eye), lenb.shape)
    loads[0].wait()
    row8 = lax.rem(lax.broadcasted_iota(jnp.int32, (16, 8 * S), 0), 8)
    lanes = lax.broadcasted_iota(jnp.int32, (16, 8 * S), 1)
    own_row = lanes // S == row8
    place = lax.rem(lanes, S).astype(F32)
    for b in range(M // 8):
        q8 = qf[8 * b:8 * b + 8, :]
        both = jnp.concatenate([q8[:, :HD], q8[:, HD:]], axis=0).astype(BF16)
        length = lenb[8 * b:8 * b + 8, :]
        length = jnp.concatenate([length, length], axis=0)
        keys = sfx[8 * b:8 * b + 8, 0].reshape(8 * S, HD)
        values = sfx[8 * b:8 * b + 8, 1].reshape(8 * S, HD)
        weights = jnp.where(own_row & (place < length), capped_exp(nt(both, keys)), 0.0)
        den = jnp.sum(weights, axis=1, keepdims=True)
        num = dot(weights.astype(BF16), values)
        for h in range(2):
            num_s[8 * b:8 * b + 8, h * HD:(h + 1) * HD] = num[8 * h:8 * h + 8, :]
            den_s[8 * b:8 * b + 8, h * HD:(h + 1) * HD] = jnp.broadcast_to(den[8 * h:8 * h + 8, :], (8, HD))
    for load in loads[1:1 + 2 * G]:
        load.wait()

    arrived(recv, rsem)
    stage[...] = recv[...].reshape(R * ROWS, 128).astype(F32)
    CH = 512
    rows, gid = [], []
    for part in range(PARTS):
        def chunk(n):
            return stage[pl.ds(part * H * ROWS + n, H, stride=ROWS), :]

        for k in range(2):
            for h in range(2):
                rows.append(jnp.concatenate([chunk(k * 4 + 2 * h), chunk(k * 4 + 2 * h + 1)], axis=1))
                gid.append(chunk(8 + k))
    rows, gid = jnp.concatenate(rows, axis=0), jnp.concatenate(gid, axis=0)
    gid2 = jnp.concatenate([gid, gid], axis=1)
    length = jnp.zeros(gid.shape, jnp.int32)
    for g in range(G):
        qsel[g] = jnp.where(gid2 == float(g), rows, 0.0).astype(BF16)
        length = jnp.where(gid == float(g), plen_ref[0:1, g:g + 1], length)
    length4 = jnp.concatenate([length] * (CH // 128), axis=1)
    total_den = jnp.zeros((4 * R, 1), F32)
    for p in range(size // CH):
        scores = nt(qsel[0], kv[0, 0, p * CH:(p + 1) * CH, :])
        for g in range(1, G):
            scores = scores + nt(qsel[g], kv[g, 0, p * CH:(p + 1) * CH, :])
        position = lax.broadcasted_iota(jnp.int32, scores.shape, 1) + p * CH
        weights = jnp.where(position < length4, capped_exp(scores), 0.0)
        total_den = total_den + jnp.sum(weights, axis=1, keepdims=True)
        wts[:, p * CH:(p + 1) * CH] = weights.astype(BF16)
    high = total_den.astype(BF16).astype(F32)
    low = total_den - high
    safe = jnp.where(total_den > 0.0, total_den, 1.0)
    quarter = lax.broadcasted_iota(jnp.int32, (H, 128), 1) // 32
    for part in range(PARTS):
        first = part * H
        these = slice(4 * first, 4 * (first + H))
        num = jnp.zeros((4 * H, HD), F32)
        for g in range(G):
            num = jnp.where(gid2[these] == float(g), dot(wts[these, :], kv[g, 1]), num)
        mean = num / safe[these]
        for k in range(2):
            dens = jnp.zeros((H, 128), F32)
            for h in range(2):
                at = slice((k * 2 + h) * H, (k * 2 + h + 1) * H)
                stage_out[pl.ds(first * ROWS + k * 4 + 2 * h, H, stride=ROWS), :] = mean[at, :128]
                stage_out[pl.ds(first * ROWS + k * 4 + 2 * h + 1, H, stride=ROWS), :] = mean[at, 128:]
                dens = jnp.where(quarter == 2 * h, high[these][at], jnp.where(quarter == 2 * h + 1, low[these][at], dens))
            stage_out[pl.ds(first * ROWS + 8 + k, H, stride=ROWS), :] = dens
        back[first:first + H] = stage_out[first * ROWS:(first + H) * ROWS, :].astype(BF16).reshape(H, ROWS, 128)
        dispatch(back, ret, bsem, tsem, behind, first, first + H)

    spot = lax.broadcasted_iota(jnp.int32, (M, 2 * R), 1).astype(F32)
    fetch = jnp.where(spot == rank_col * float(R) + o_col, 1.0, 0.0).astype(BF16)
    loads[1 + 2 * G].wait()
    loads[2 + 2 * G].wait()
    loads[3 + 2 * G].wait()
    arrived(ret, tsem)
    stage[...] = ret[...].reshape(R * ROWS, 128).astype(F32)

    def answers(n):
        return stage[pl.ds(n, R, stride=ROWS), :]

    table = jnp.concatenate(
        [jnp.concatenate([answers(n) for n in (k * 4, k * 4 + 1, k * 4 + 2, k * 4 + 3, 8 + k)], axis=1) for k in range(2)], axis=0
    ).astype(BF16)
    mine = dot(fetch, table)
    parts = []
    for h in range(2):
        den_p = mine[:, 512 + 64 * h:513 + 64 * h] + mine[:, 544 + 64 * h:545 + 64 * h]
        cols = slice(h * HD, (h + 1) * HD)
        parts.append((mine[:, cols] * den_p + num_s[:, cols]) / (den_p + den_s[:, cols]))
    attention = jnp.concatenate(parts, axis=1).astype(BF16)

    atts[0] = attention
    given = []
    for off in (1, 3):
        given.append(pltpu.make_async_remote_copy(
            src_ref=atts.at[0], dst_ref=atts.at[T - off], send_sem=psem.at[off], recv_sem=prsem.at[T - off],
            device_id=(me, lax.rem(t + off, T)), device_id_type=MESH,
        ))
        given[-1].start()
    far[0] = dot(attention, wcol[2]).astype(BF16)
    given.append(pltpu.make_async_remote_copy(
        src_ref=far.at[0], dst_ref=far.at[1], send_sem=psem.at[2], recv_sem=prsem.at[2],
        device_id=(me, lax.rem(t + 2, T)), device_id_type=MESH,
    ))
    given[-1].start()
    passed = []
    for off in (1, 3):
        pltpu.make_async_copy(wcol.at[off, my_rows], wcol.at[off, my_rows], wrsem.at[off]).wait()
        passed.append(pltpu.make_async_remote_copy(
            src_ref=wcol.at[off, my_rows], dst_ref=wcol.at[off, my_rows], send_sem=fsem.at[off], recv_sem=frsem.at[off],
            device_id=(sibling, t), device_id_type=MESH,
        ))
        passed[-1].start()
    total = dot(attention, wcol[0])
    for n, off in enumerate((1, 3)):
        passed[n].wait_recv()
        pltpu.make_async_copy(atts.at[off], atts.at[off], prsem.at[off]).wait()
        total = total + dot(atts[off], wcol[off])
    given[-1].wait_recv()
    total = total + far[1].astype(F32)

    square = jnp.sum(total * total, axis=1, keepdims=True)
    eye_wide = lax.broadcasted_iota(jnp.int32, (M, 128), 0) == lax.broadcasted_iota(jnp.int32, (M, 128), 1)
    square_row = jnp.sum(jnp.where(eye_wide, square, 0.0), axis=0, keepdims=True)
    sqsend[...] = jnp.broadcast_to(square_row, (8, 128))
    squares = []
    for off in (2, 1, 3):
        squares.append(pltpu.make_async_remote_copy(
            src_ref=sqsend, dst_ref=sqrecv.at[off], send_sem=qsem.at[off], recv_sem=qrsem.at[off],
            device_id=(me, lax.rem(t + off, T)), device_id_type=MESH,
        ))
        squares[-1].start()
    scaled = total * gain_ref[...].reshape(1, width)
    departed(send, ssem)
    departed(back, bsem)
    for copy in squares:
        copy.wait_recv()
    for off in range(1, T):
        square_row = square_row + sqrecv[off, 0:1, :]
    mean_square = column(square_row, eye_wide) * (1.0 / (width * T))
    out_ref[...] = (hid[...].astype(F32) + scaled * lax.rsqrt(mean_square + EPSILON)).astype(BF16)

    for copy in weights_out + given + passed + squares:
        copy.wait_send()


def shards(
    hidden_input, queries, prompt_cache, suffix_cache, owner_replica, group_slot, prompt_length, suffix_length,
    output_weight, post_gain,
):
    R, T = lax.axis_size("replica"), lax.axis_size("tensor")
    M, width = hidden_input.shape
    G, _, size, _ = prompt_cache.shape
    S = suffix_cache.shape[2]
    vmem = pl.BlockSpec(memory_space=pltpu.VMEM)
    hbm = pl.BlockSpec(memory_space=pl.ANY)
    dma = pltpu.SemaphoreType.DMA
    message = pltpu.VMEM((R, ROWS, 128), BF16)
    result = pl.pallas_call(
        functools.partial(kernel, R, T, M, width),
        out_shape=pltpu.VMEM((M, width), BF16),
        in_specs=[hbm] * 10,
        out_specs=vmem,
        scratch_shapes=[
            pltpu.VMEM((1, M), jnp.int32), pltpu.VMEM((1, M), jnp.int32), pltpu.VMEM((1, M), jnp.int32), pltpu.VMEM((1, G), jnp.int32),
            pltpu.VMEM((width,), F32), pltpu.VMEM(queries.shape, BF16),
            pltpu.VMEM(prompt_cache.shape, BF16),
            pltpu.VMEM(suffix_cache.shape, BF16),
            pltpu.VMEM((T, output_weight.shape[0], width), BF16),
            pltpu.VMEM((M, width), BF16),
            message, message, message, message,
            pltpu.VMEM((R * ROWS, 128), F32),
            pltpu.VMEM((R * ROWS, 128), F32),
            pltpu.VMEM((M, 2 * HD), F32),
            pltpu.VMEM((M, 8 * S), F32),
            pltpu.VMEM((G, 4 * R, HD), BF16),
            pltpu.VMEM((4 * R, size), BF16),
            pltpu.VMEM((M, 2 * HD), F32),
            pltpu.VMEM((M, 2 * HD), F32),
            pltpu.VMEM((T, M, 2 * HD), BF16),
            pltpu.VMEM((2, M, width), BF16),
            pltpu.VMEM((8, 128), F32),
            pltpu.VMEM((T, 8, 128), F32),
            dma((6,)), dma((4 + 2 * G,)), dma(()), dma(()), dma(()), dma(()), *[dma((T,))] * 8,
        ],
        compiler_params=pltpu.CompilerParams(collective_id=0, has_side_effects=True, vmem_limit_bytes=56 * 2 ** 20),
        name="decode_attention",
    )(
        owner_replica.reshape(1, M), group_slot.reshape(1, M), suffix_length.reshape(1, M), prompt_length.reshape(1, G),
        post_gain, queries, hidden_input, prompt_cache, suffix_cache, output_weight,
    )

    return result


def solution(mesh):
    in_specs = (
        P("replica", "tensor"), P("replica", "tensor"), P("replica", None, None, "tensor"), P("replica", None, None, "tensor"),
        P("replica", None), P("replica"), P("replica"), P("replica"), P("tensor", None), P("tensor"),
    )
    return jax.shard_map(shards, mesh=mesh, in_specs=in_specs, out_specs=P("replica", "tensor"), check_vma=False)
```
